256 devices in a mesh: gx: 32 (over x, z), gy: 8 (over y, core).
Axes of the slice: x: 4, y: 4, z: 8, core: 2. Of those that a mesh axis runs over, the one named last changes fastest.
Arguments:
- spheres: float32 [13, 8, 256, 128], P(None, 'gy', 'gx')
- new_home: int32 [8, 256], P('gy', 'gx'), may hold values from 0 to 255, as said below
- ghost_list: int32 [8, 64], P('gy', 'gx'), may hold values from 0 to 7, as said below
- tile_pairs: int32 [8, 8192, 2], P('gy', 'gx'), may hold values from 0 to 25, as said below
- tile_count: int32 [8, 32], P('gy', 'gx'), may hold values from 24 to 256
Outputs:
- updated: float32 [13, 8, 256, 128], P(None, 'gy', 'gx')
The draws below stay inside these ranges and needn't reach their ends.
Inputs may be any that keep to these rules, and one draw needn't show every extreme that they name: Within each row new_home is a permutation of the row's slots; a block in slot b moves to the device 0 to 3 slabs ahead along gx, cyclically; some block moves exactly 3 slabs. `ghost_list`: the 2 entries of one device are distinct. `tile_pairs`: column 0 is a local block; column 1 is a pool entry below 16 or from 18 on; every such pool entry appears in a valid tile of every device.
All inputs are finite; a program needn't handle non-finite values.
Results may differ from the reference program's by a relative error of at most 0.0003.
Values sent between devices are 32-bit elements; how exact they have to be, the bound alone decides.
No kernel may reach another device: no remote copies, remote signals or barrier semaphores. Data moves between devices by JAX's collectives and lax.ppermute only.
A program may use at most 64 MiB of HBM per device.

```python
import jax
import jax.numpy as jnp
from jax import lax

BLOCK = 128
DEVICE_BLOCKS = 8
GHOST = 2
TILE_CAP = 256
N_GX = 32
N_GY = 8


def draw_spheres(key, part):
    random_keys = jax.random.split(key, 5)
    shape_one = (N_GY, N_GX * DEVICE_BLOCKS, BLOCK)
    position = jax.random.uniform(random_keys[0], (3,) + shape_one, dtype=jnp.float32)
    velocity = jax.random.normal(random_keys[1], (3,) + shape_one)
    angular = 3.0 * jax.random.normal(random_keys[2], (3,) + shape_one)
    accel = 2.0 * jax.random.normal(random_keys[3], (3,) + shape_one)
    radius = jax.random.uniform(random_keys[4], (1,) + shape_one, minval=0.08, maxval=0.12)
    return jnp.concatenate([position, velocity, angular, accel, radius], 0).astype(jnp.float32)


def draw_new_home(key, part):
    slab_windows = N_GX // 2
    pair_len = 2 * DEVICE_BLOCKS
    random_keys = jax.random.split(key, N_GY * slab_windows + N_GY)

    def one_window(wkey):
        perm = jax.random.permutation(wkey, pair_len)
        final_position = jnp.argmax(perm == pair_len - 1)
        perm = perm.at[final_position].set(perm[0])
        return perm.at[0].set(pair_len - 1)
    perms = jax.vmap(one_window)(random_keys[:N_GY * slab_windows]).reshape(N_GY, slab_windows, pair_len)
    base = (jnp.arange(slab_windows, dtype=jnp.int32) * pair_len)[None, :, None]
    slab_offsets = jax.vmap(lambda sphere_key: jax.random.randint(sphere_key, (), 1, DEVICE_BLOCKS))(random_keys[N_GY * slab_windows:])
    home = (perms + base).reshape(N_GY, N_GX * DEVICE_BLOCKS) + (slab_offsets + DEVICE_BLOCKS)[:, None]
    return (home % (N_GX * DEVICE_BLOCKS)).astype(jnp.int32)


def draw_ghost_list(key, part):
    random_keys = jax.random.split(key, N_GY * N_GX)
    picks = jax.vmap(lambda gkey: jax.random.permutation(gkey, DEVICE_BLOCKS)[:GHOST])(random_keys)
    return picks.reshape(N_GY, N_GX * GHOST).astype(jnp.int32)


def draw_tile_pairs(key, part):
    valid_pool = DEVICE_BLOCKS + 8 * GHOST
    random_keys = jax.random.split(key, N_GY * N_GX)

    def one_device(dkey):
        first, second, third = jax.random.split(dkey, 3)
        left_idx = jax.random.randint(first, (TILE_CAP,), 0, DEVICE_BLOCKS)
        entry = jnp.concatenate([jax.random.permutation(second, valid_pool), jax.random.randint(third, (TILE_CAP - valid_pool,), 0, valid_pool)])
        right_idx = jnp.where(entry < DEVICE_BLOCKS + 4 * GHOST, entry, entry + GHOST)
        return jnp.stack([left_idx, right_idx], 1)
    pairs = jax.vmap(one_device)(random_keys)
    return pairs.reshape(N_GY, N_GX * TILE_CAP, 2).astype(jnp.int32)


def draw_tile_count(key, part):
    valid_pool = DEVICE_BLOCKS + 8 * GHOST
    random_keys = jax.random.split(key, 4)
    spread = TILE_CAP - valid_pool + 1
    first = jax.random.randint(random_keys[0], (N_GY * N_GX,), 0, spread)
    second = jax.random.randint(random_keys[1], (N_GY * N_GX,), 0, spread)
    third = jax.random.randint(random_keys[2], (N_GY * N_GX,), 0, spread)
    counts = valid_pool + jnp.minimum(jnp.minimum(first, second), third)
    chosen = jax.random.randint(random_keys[3], (), 0, N_GY * N_GX)
    counts = counts.at[chosen].set(TILE_CAP)
    counts = counts.at[(chosen + 1) % (N_GY * N_GX)].set(valid_pool)
    return counts.reshape(N_GY, N_GX).astype(jnp.int32)


def setup_inputs(seed: int = 0) -> dict:
    keys = jax.random.split(jax.random.key(seed), 6)
    spheres = draw_spheres(jax.random.fold_in(keys[5], 71), 0)
    new_home = draw_new_home(jax.random.fold_in(keys[5], 71), 0)
    ghost_list = draw_ghost_list(jax.random.fold_in(keys[5], 71), 0)
    tile_pairs = draw_tile_pairs(jax.random.fold_in(keys[5], 71), 0)
    tile_count = draw_tile_count(jax.random.fold_in(keys[5], 71), 0)
    return {"spheres": spheres, "new_home": new_home, "ghost_list": ghost_list, "tile_pairs": tile_pairs, "tile_count": tile_count}


time_step = 0.01
stiffness = 200.0
damp_normal = 20.0
damp_tangent = 10.0
cohesion = 10.0
density = 240.0

def cross_three(left, right):
    return jnp.stack([left[1] * right[2] - left[2] * right[1], left[2] * right[0] - left[0] * right[2], left[0] * right[1] - left[1] * right[0]], 0)

def contact(part_left, right_particle, same_block):
    width = part_left.shape[1]
    sep = part_left[0:3, :, None] - right_particle[0:3, None, :]
    dist = jnp.sqrt(lax.optimization_barrier(jnp.sum(sep * sep, 0)))
    rad_left = part_left[12][:, None]
    rad_right = right_particle[12][None, :]
    depth = rad_left + rad_right - dist
    diagonal = jnp.eye(width, dtype=bool)
    touch = (depth > 0) & jnp.logical_not(same_block & diagonal)
    safe_dist = jnp.where(touch, dist, 1.0)
    normal = jnp.where(touch[None], sep / safe_dist[None], 0.0)
    depth = jnp.where(touch, depth, 0.0)
    reduced = rad_left * rad_right / (rad_left + rad_right)
    contact_rad = jnp.sqrt(reduced * depth)
    spin = part_left[6:9, :, None] * rad_left[None] + right_particle[6:9, None, :] * rad_right[None]
    relative = part_left[3:6, :, None] - right_particle[3:6, None, :] - cross_three(spin, normal)
    normal_speed = lax.optimization_barrier(jnp.sum(relative * normal, 0))
    tangent = relative - normal_speed[None] * normal
    normal_force = stiffness * contact_rad * depth - damp_normal * contact_rad * normal_speed - cohesion * contact_rad
    tangent_force = -damp_tangent * contact_rad[None] * tangent
    force = lax.optimization_barrier(jnp.sum(normal_force[None] * normal + tangent_force, 2))
    torque = lax.optimization_barrier(jnp.sum(-rad_left[None] * cross_three(normal, tangent_force), 2))
    return jnp.concatenate([force, torque], 0)

def advance(drifted, forces_sum):
    radius = drifted[12:13]
    mass = density * (4.0 / 3.0) * jnp.pi * radius ** 3
    inertia = 0.4 * mass * radius * radius
    gravity_vec = jnp.array([0.0, 0.0, -1.0], dtype=drifted.dtype).reshape((3,) + (1,) * (drifted.ndim - 1))
    accel = forces_sum[0:3] / mass + gravity_vec
    velocity = drifted[3:6] + 0.5 * time_step * (drifted[9:12] + accel)
    angular = drifted[6:9] + time_step * forces_sum[3:6] / inertia
    return jnp.concatenate([drifted[0:3], velocity, angular, accel, radius], 0)

def reference(spheres, new_home, ghost_list, tile_pairs, tile_count):

    def move_row(row_data, row_home):
        return jnp.zeros_like(row_data).at[:, row_home].add(row_data)
    moved_blocks = jax.vmap(move_row, in_axes=(1, 0), out_axes=1)(spheres, new_home)
    position = moved_blocks[0:3] + time_step * moved_blocks[3:6] + 0.5 * time_step * time_step * moved_blocks[9:12]
    drifted = jnp.concatenate([position, moved_blocks[3:]], 0)
    grid = drifted.reshape(13, N_GY, N_GX, DEVICE_BLOCKS, BLOCK)
    picks = ghost_list.reshape(N_GY, N_GX, GHOST).astype(jnp.int32)
    picks = jnp.broadcast_to(picks[None, :, :, :, None], (13, N_GY, N_GX, GHOST, BLOCK))
    ghosts = jnp.take_along_axis(grid, picks, axis=3)
    shells = []
    for row_step in (-1, 0, 1):
        for col_step in (-1, 0, 1):
            shells.append(jnp.roll(ghosts, (-row_step, -col_step), axis=(1, 2)))
    shell_all = jnp.stack(shells, 3).reshape(13, N_GY, N_GX, 9 * GHOST, BLOCK)
    pool_all = jnp.concatenate([grid, shell_all], 3)
    pool_entries = DEVICE_BLOCKS + 9 * GHOST
    pool_dev = pool_all.transpose(1, 2, 0, 3, 4).reshape(N_GY * N_GX, 13, pool_entries, BLOCK)
    pairs_dev = tile_pairs.reshape(N_GY * N_GX, TILE_CAP, 2)
    counts_dev = tile_count.reshape(N_GY * N_GX)

    def one_device(inputs):
        pool_one, pairs_one, count_one = inputs

        def tile_step(index, forces_sum):
            left_idx = pairs_one[index, 0]
            right_idx = pairs_one[index, 1]
            terms = contact(pool_one[:, left_idx], pool_one[:, right_idx], left_idx == right_idx)
            return forces_sum.at[:, left_idx].add(terms)
        start = jnp.zeros((6, DEVICE_BLOCKS, BLOCK), dtype=pool_one.dtype)
        return lax.fori_loop(0, count_one, tile_step, start)
    totals = lax.map(one_device, (pool_dev, pairs_dev, counts_dev))
    totals = totals.reshape(N_GY, N_GX, 6, DEVICE_BLOCKS, BLOCK).transpose(2, 0, 1, 3, 4)
    totals = totals.reshape(6, N_GY, N_GX * DEVICE_BLOCKS, BLOCK)
    return advance(drifted, totals)
```

```python
import jax
import jax.numpy as jnp
from jax import lax
from jax.experimental import pallas as pl
from jax.experimental.pallas import tpu as pltpu
from jax.sharding import PartitionSpec as P

SPAN = 3
DT = 0.01
DENSITY = 240.0
SC = 20.0
NB = 8
NP = 26
NT = NB * NP
U = 4
FLAGS = None

f32 = jnp.float32
bf16 = jnp.bfloat16
i32 = jnp.int32


def passed_along(x, axis, by):
    peers = lax.axis_size(axis)
    return lax.ppermute(x, axis, [(i, (i + by) % peers) for i in range(peers)])


def pack_kernel(home_ref, me_ref, x_ref, b0, b1, b2, b3, buf):
    buf[...] = jnp.zeros_like(buf)
    for b in range(NB):
        home = home_ref[0, b]
        ahead = (home // NB - me_ref[0] + 32) % 32
        buf[ahead, :, pl.ds(home % NB, 1), :] = x_ref[:, b : b + 1, :]
    for k, out in enumerate((b0, b1, b2, b3)):
        out[...] = buf[k]


def drift_kernel(lent_ref, a0, a1, a2, a3, drifted, lent):
    x = a0[...] + a1[...] + a2[...] + a3[...]
    drifted[3:13] = x[3:13]
    drifted[0:3] = x[0:3] + DT * x[3:6] + (0.5 * DT * DT) * x[9:12]
    for q in range(2):
        slot = lent_ref[0, q]
        for c in range(13):
            lent[q, c : c + 1, :] = drifted[c, pl.ds(slot, 1), :]
        lent[q, 13:16, :] = jnp.zeros((3, 128), f32)


def split3(f):
    h = f.astype(bf16)
    r = f - h.astype(f32)
    m = r.astype(bf16)
    return h, m, (r - m.astype(f32)).astype(bf16)


def cross(a, b):
    return [
        a[1] * b[2] - a[2] * b[1],
        a[2] * b[0] - a[0] * b[2],
        a[0] * b[1] - a[1] * b[0],
    ]


def dot3(a, b):
    return a[0] * b[0] + a[1] * b[1] + a[2] * b[2]


def scaled(get):
    x = [get(c) * SC for c in range(3)]
    v = [get(3 + c) for c in range(3)]
    r = get(12)
    u = [r * get(6 + c) for c in range(3)]
    return x, v, u, r * SC


def left_prep(get, ab, la):
    x, v, u, rp = scaled(get)
    zero = jnp.zeros_like(rp)
    rows = x + v + u + [dot3(x, v), dot3(x, u), jnp.ones_like(rp), rp, zero, zero, zero]
    pad = jnp.zeros((112, 128), f32)
    for i in range(NB):
        f = jnp.concatenate([q[i : i + 1] for q in rows], 0)
        t = jnp.concatenate([f, pad], 0).T
        for n, c in enumerate((0, 1, 2, 12)):
            ab[i, n] = jnp.broadcast_to(t[:, c : c + 1], (128, 128))
        a = lax.broadcasted_iota(i32, (128, 128), 0)
        b = lax.broadcasted_iota(i32, (128, 128), 1)
        ab[i, 4] = jnp.where(a == b, 1e15, jnp.broadcast_to(t[:, 0:1], (128, 128)))
        h, m, l = (p.astype(f32) for p in split3(f))
        la[i] = jnp.concatenate([h, h, m, m, h, l, pad[:32]], 0).T.astype(bf16)


def right_rows(get):
    x, v, u, rp = scaled(get)
    one = jnp.ones_like(rp)
    zero = jnp.zeros_like(rp)
    neg = lambda a: [-q for q in a]
    s = neg(v) + neg(x) + [zero] * 3 + [one, zero, dot3(x, v)] + [zero] * 4
    t = u + [zero] * 3 + neg(x) + [zero, one, -dot3(x, u)] + [zero] * 4
    sb = jnp.sqrt(rp)
    w = [sb * q for q in [one] + x + v + u + cross(u, x) + cross(x, v)]
    return x + [rp], s, t, w


def right_store(rows, s, t, w, rb, kb, wb, j):
    rb[j, 0:4] = rows
    sh, sm, sl = split3(s)
    th, tm, tl = split3(t)
    for n, (p, q) in enumerate(((sh, th), (sm, tm), (sh, th), (sm, tm), (sl, tl), (sh, th))):
        kb[j, 16 * n : 16 * n + 16, 0:128] = p
        kb[j, 16 * n : 16 * n + 16, 128:256] = q
    kb[j, 96:128, :] = jnp.zeros((32, 256), bf16)
    for n, p in enumerate(split3(w)):
        wb[j, 16 * n : 16 * n + 16, 0:128] = p
        wb[j, 16 * n : 16 * n + 16, 128:256] = p


def tile_dots(i, j, la, kb, st):
    st[...] = jnp.dot(la[i], kb[j], preferred_element_type=f32)


def tile_terms(i, j, ab, st, rb, cf):
    xi = jnp.where(i == j, 4, 0)
    rows = 16
    right = [jnp.broadcast_to(rb[j, q : q + 1, :], (rows, 128)) for q in range(4)]
    for c in range(128 // rows):
        sl = slice(rows * c, rows * c + rows)
        dx = ab[i, xi, sl, :] - right[0]
        dy = ab[i, 1, sl, :] - right[1]
        dz = ab[i, 2, sl, :] - right[2]
        rs = ab[i, 3, sl, :] + right[3]
        d2 = jnp.minimum(dx * dx + dy * dy + dz * dz, 1e37)
        inv = lax.rsqrt(d2)
        depth = jnp.maximum(rs - d2 * inv, 0.0)
        rc = depth * lax.rsqrt(jnp.maximum(depth * rs, 1e-35))
        ga = rc * inv
        gi = ga * inv
        al = ga * depth - gi * st[sl, 0:128]
        de = gi * st[sl, 128:256]
        for n, co in enumerate((al, rc, ga, de)):
            h = co.astype(bf16)
            cf[128 * n + rows * c : 128 * n + rows * c + rows, 0:128] = h
            cf[128 * n + rows * c : 128 * n + rows * c + rows, 128:256] = (
                co - h.astype(f32)
            ).astype(bf16)


def tile_sums(i, j, mult, wb, cf, acc):
    o = lax.dot_general(
        wb[j], cf[...], (((1,), (1,)), ((), ())), preferred_element_type=f32
    )
    acc[i] += (o[0:16] + o[16:32] + o[32:48]) * mult


def tile_loop(start, stop, list_ref, ab, la, rb, kb, wb, cfs, sts, acc):
    def get(e):
        code = list_ref[0, e]
        return code & 7, code >> 3, list_ref[1, e].astype(f32)

    trips = (stop - start + U - 1) // U
    for cf in cfs:
        cf[...] = jnp.zeros_like(cf)
    for n in range(U):
        i, j, _ = get(start + n)
        tile_dots(i, j, la, kb, sts[n])

    def body(t, prev):
        base = start + U * t
        cur = [get(base + n) for n in range(U)]
        for n in range(U):
            i, j, mult = prev[n]
            tile_sums(i, j, mult, wb, cfs[n], acc)
        for n in range(U):
            i, j, _ = cur[n]
            tile_terms(i, j, ab, sts[n], rb, cfs[n])
        for n in range(U):
            i, j, _ = get(base + U + n)
            tile_dots(i, j, la, kb, sts[n])
        return tuple(cur)

    none = (jnp.int32(0), jnp.int32(0), jnp.float32(0))
    prev = lax.fori_loop(0, trips, body, (none,) * U)
    for n in range(U):
        i, j, mult = prev[n]
        tile_sums(i, j, mult, wb, cfs[n], acc)


def finish(d, acc, out):
    sums = [[None] * 16 for _ in range(4)]
    need = ((0, 4), (0, 10), (0, 16), (0, 4))
    for q in range(4):
        for r in range(need[q][1]):
            sums[q][r] = jnp.concatenate(
                [acc[i, r : r + 1, 128 * q : 128 * q + 128] for i in range(NB)], 0
            )
    a, b, g, e = sums
    x, v, u, rp = scaled(lambda c: d[c])
    uxg = cross(u, g[1:4])
    ux = cross(u, x)
    gux = cross(g[7:10], x)
    xv = cross(x, v)
    xgv = cross(x, g[4:7])
    gxv = cross(g[1:4], v)
    r = d[12]
    mass = (DENSITY * (4.0 / 3.0) * jnp.pi) * (r * r * r)
    inertia = 0.4 * mass * r * r
    half = 0.5 * jnp.sqrt(rp)
    to_acc = half / mass
    to_ang = half * r * DT / inertia
    for c in range(3):
        force = (
            x[c] * (a[0] - g[0])
            - (a[1 + c] - g[1 + c])
            - (v[c] * b[0] - b[4 + c])
            + (ux[c] * g[0] - uxg[c] + gux[c] - g[10 + c])
        )
        torque = (
            (xv[c] * g[0] - xgv[c] - gxv[c] + g[13 + c])
            - (u[c] * b[0] + b[7 + c])
            + (x[c] * e[0] - e[1 + c])
        )
        accel = force * to_acc
        if c == 2:
            accel = accel - 1.0
        out[c] = d[c]
        out[3 + c] = v[c] + (0.5 * DT) * (d[9 + c] + accel)
        out[6 + c] = d[6 + c] + torque * to_ang
        out[9 + c] = accel
    out[12] = r


def step_kernel(list_ref, n_ref, d, ghosts, out, ab, la, rb, kb, wb, acc, *bufs):
    acc[...] = jnp.zeros_like(acc)
    left_prep(lambda c: d[c], ab, la)
    rows = right_rows(lambda c: d[c])
    for j in range(NB):
        right_store(*(jnp.concatenate([q[j : j + 1] for q in p], 0) for p in rows), rb, kb, wb, j)
    for lo in range(0, 18, 6):
        rows = right_rows(
            lambda c: jnp.concatenate([ghosts[lo + q, c : c + 1, :] for q in range(6)], 0)
        )
        for q in range(6):
            right_store(
                *(jnp.concatenate([f[q : q + 1] for f in p], 0) for p in rows),
                rb, kb, wb, NB + lo + q,
            )
    tile_loop(jnp.int32(0), n_ref[0], list_ref, ab, la, rb, kb, wb, bufs[:U], bufs[U:], acc)
    finish(d, acc, out)


VM = pl.BlockSpec(memory_space=pltpu.VMEM)
SM = pl.BlockSpec(memory_space=pltpu.SMEM)


def shaped(*shape):
    return jax.ShapeDtypeStruct(shape, f32)


def tile_list(pairs, count):
    valid = jnp.arange(256) < count
    code = jnp.where(valid, pairs[:, 1] * NB + pairs[:, 0], 255)
    codes = jnp.arange(256)
    often = jnp.sum((code[:, None] == codes[None, :]).astype(i32), 0)
    often = jnp.where(codes < NT, often, 0)
    there = often > 0
    rank = jnp.sum((there[:, None] & (codes[:, None] < codes[None, :])).astype(i32), 0)
    pick = there[:, None] & (rank[:, None] == codes[None, :])
    order = jnp.sum(jnp.where(pick, codes[:, None], 0), 0)
    times = jnp.sum(jnp.where(pick, often[:, None], 0), 0)
    return jnp.stack([order, times], 0), jnp.sum(there.astype(i32))[None]


def per_device(spheres, new_home, ghost_list, tile_pairs, tile_count):
    local = spheres.reshape(13, NB, 128)
    me = lax.axis_index("gx").astype(i32)[None]
    block = shaped(13, NB, 128)
    bufs = pl.pallas_call(
        pack_kernel,
        out_shape=(block,) * 4,
        in_specs=[SM, SM, VM],
        out_specs=(VM,) * 4,
        scratch_shapes=[pltpu.VMEM((4, 13, NB, 128), f32)],
        name="pack",
    )(new_home, me, local)
    came = [passed_along(bufs[k], "gx", k) for k in range(1, SPAN + 1)]
    order, total = tile_list(tile_pairs[0], tile_count[0, 0])
    drifted, lent = pl.pallas_call(
        drift_kernel,
        out_shape=(block, shaped(2, 16, 128)),
        in_specs=[SM, VM, VM, VM, VM],
        out_specs=(VM, VM),
        name="drift",
    )(ghost_list, bufs[0], *came)
    behind = passed_along(lent, "gx", 1)
    front = passed_along(lent, "gx", -1)
    line = jnp.concatenate([behind, lent, front], 0)
    below = passed_along(line, "gy", 1)
    above = passed_along(line, "gy", -1)
    ghosts = jnp.concatenate([below, line, above], 0)
    out = pl.pallas_call(
        step_kernel,
        out_shape=block,
        in_specs=[SM, SM, VM, VM],
        out_specs=VM,
        scratch_shapes=[
            pltpu.VMEM((NB, 5, 128, 128), f32),
            pltpu.VMEM((NB, 128, 128), bf16),
            pltpu.VMEM((NP, 8, 128), f32),
            pltpu.VMEM((NP, 128, 256), bf16),
            pltpu.VMEM((NP, 48, 256), bf16),
            pltpu.VMEM((NB, 16, 512), f32),
        ]
        + [pltpu.VMEM((512, 256), bf16)] * U
        + [pltpu.VMEM((128, 256), f32)] * U,
        compiler_params=pltpu.CompilerParams(flags=FLAGS),
        name="step",
    )(order, total, drifted, ghosts)
    return out[:, None]


def solution(mesh):
    in_specs = (
        P(None, "gy", "gx", None),
        P("gy", "gx"),
        P("gy", "gx"),
        P("gy", "gx", None),
        P("gy", "gx"),
    )
    return jax.shard_map(
        per_device,
        mesh=mesh,
        in_specs=in_specs,
        out_specs=P(None, "gy", "gx", None),
        check_vma=False,
    )
```

```python
import jax
import jax.numpy as jnp
from jax import lax
from jax.experimental import pallas as pl
from jax.experimental.pallas import tpu as pltpu
from jax.sharding import PartitionSpec as P

SPAN = 3
DT = 0.01
DENSITY = 240.0
SC = 20.0
NB = 8
NP = 26
NT = NB * NP
U = 4
FLAGS = None

f32 = jnp.float32
bf16 = jnp.bfloat16
i32 = jnp.int32


def passed_along(x, axis, by):
    peers = lax.axis_size(axis)
    return lax.ppermute(x, axis, [(i, (i + by) % peers) for i in range(peers)])


def pack_kernel(home_ref, me_ref, x_ref, b0, b1, b2, b3, buf):
    buf[...] = jnp.zeros_like(buf)
    for b in range(NB):
        home = home_ref[0, b]
        ahead = ((home >> 3) - me_ref[0]) & 31
        buf[ahead, :, pl.ds(home & 7, 1), :] = x_ref[:, b : b + 1, :]
    for k, out in enumerate((b0, b1, b2, b3)):
        out[...] = buf[k]


def list_kernel(count_ref, pairs_ref, out):
    lane = lax.broadcasted_iota(i32, (1, 256), 1)
    code = jnp.where(lane < count_ref[0, 0], pairs_ref[1:2, :] * NB + pairs_ref[0:1, :], 255)
    rows = 224
    c = lax.broadcasted_iota(i32, (rows, 256), 0)
    hit = jnp.where(code == c, 1.0, 0.0).astype(bf16)
    often = jnp.dot(hit, jnp.ones((256, 128), bf16), preferred_element_type=f32)
    ci = lax.broadcasted_iota(i32, (rows, 128), 0)
    there = (often > 0.5) & (ci < NT)
    r = lax.broadcasted_iota(i32, (rows, rows), 0)
    q = lax.broadcasted_iota(i32, (rows, rows), 1)
    rank = jnp.dot(
        jnp.where(q < r, 1.0, 0.0).astype(bf16),
        jnp.where(there, 1.0, 0.0).astype(bf16),
        preferred_element_type=f32,
    )
    cf = ci.astype(f32)
    for half in range(2):
        e = lax.broadcasted_iota(i32, (rows, 128), 1).astype(f32) + 128.0 * half
        pick = there & (rank == e)
        sl = slice(128 * half, 128 * half + 128)
        out[0:1, sl] = jnp.sum(jnp.where(pick, cf, 0.0), 0, keepdims=True).astype(i32)
        out[1:2, sl] = jnp.sum(jnp.where(pick, often, 0.0), 0, keepdims=True).astype(i32)
        out[2:3, sl] = rank[64:65].astype(i32)
        out[3:4, sl] = rank[NT : NT + 1].astype(i32)


def drift_kernel(lent_ref, a0, a1, a2, a3, drifted, lent):
    x = a0[...] + a1[...] + a2[...] + a3[...]
    drifted[3:13] = x[3:13]
    drifted[0:3] = x[0:3] + DT * x[3:6] + (0.5 * DT * DT) * x[9:12]
    for q in range(2):
        slot = lent_ref[0, q]
        for c in range(13):
            lent[16 * q + c : 16 * q + c + 1, :] = drifted[c, pl.ds(slot, 1), :]
        lent[16 * q + 13 : 16 * q + 16, :] = jnp.zeros((3, 128), f32)


def split3(f):
    h = f.astype(bf16)
    r = f - h.astype(f32)
    m = r.astype(bf16)
    return h, m, (r - m.astype(f32)).astype(bf16)


def cross(a, b):
    return [
        a[1] * b[2] - a[2] * b[1],
        a[2] * b[0] - a[0] * b[2],
        a[0] * b[1] - a[1] * b[0],
    ]


def dot3(a, b):
    return a[0] * b[0] + a[1] * b[1] + a[2] * b[2]


def scaled(get):
    x = [get(c) * SC for c in range(3)]
    v = [get(3 + c) for c in range(3)]
    r = get(12)
    u = [r * get(6 + c) for c in range(3)]
    return x, v, u, r * SC


def left_prep(get, ab, la, feat):
    x, v, u, rp = scaled(get)
    zero = jnp.zeros_like(rp)
    rows = x + v + u + [dot3(x, v), dot3(x, u), jnp.ones_like(rp), rp, zero, zero, zero]
    for n, q in enumerate(rows):
        feat[pl.ds(n, NB, stride=16), :] = q
    a = lax.broadcasted_iota(i32, (128, 128), 0)
    b = lax.broadcasted_iota(i32, (128, 128), 1)
    for i in range(NB):
        f = feat[16 * i : 16 * i + 16, :]
        h, m, l = (p.astype(f32) for p in split3(f))
        t = jnp.concatenate([h, h, m, m, h, l, f, jnp.zeros((16, 128), f32)], 0).T
        la[i] = jnp.where(b < 96, t, 0.0).astype(bf16)
        for n, c in enumerate((96, 97, 98, 108)):
            ab[i, n] = jnp.broadcast_to(t[:, c : c + 1], (128, 128))
        ab[i, 4] = jnp.where(a == b, 1e15, jnp.broadcast_to(t[:, 96:97], (128, 128)))


def right_prep(get, nb, at, rb, kb, wb, feat):
    x, v, u, rp = scaled(get)
    one = jnp.ones_like(rp)
    zero = jnp.zeros_like(rp)
    neg = lambda a: [-q for q in a]
    sb = jnp.sqrt(rp)
    s = neg(v) + neg(x) + [zero] * 3 + [one, zero, dot3(x, v)]
    t = u + [zero] * 3 + neg(x) + [zero, one, -dot3(x, u)]
    w = [sb * q for q in [one] + x + v + u + cross(u, x) + cross(x, v)]
    for k, rows in enumerate((s, t, w, x + [rp])):
        for n in range(16 if k < 3 else 4):
            feat[pl.ds(128 * k + n, nb, stride=16), :] = rows[n] if n < len(rows) else zero
    for p in range(nb):
        j = at[p]
        fs, ft, fw = (feat[128 * k + 16 * p : 128 * k + 16 * p + 16, :] for k in range(3))
        rb[j] = feat[384 + 16 * p : 384 + 16 * p + 8, :]
        sh, sm, sl = split3(fs)
        th, tm, tl = split3(ft)
        for n, (p0, p1) in enumerate(
            ((sh, th), (sm, tm), (sh, th), (sm, tm), (sl, tl), (sh, th))
        ):
            kb[j, 16 * n : 16 * n + 16, 0:128] = p0
            kb[j, 16 * n : 16 * n + 16, 128:256] = p1
        kb[j, 96:128, :] = jnp.zeros((32, 256), bf16)
        for n, p0 in enumerate(split3(fw)):
            wb[j, 16 * n : 16 * n + 16, 0:128] = p0
            wb[j, 16 * n : 16 * n + 16, 128:256] = p0


def tile_dots(i, j, la, kb, st):
    st[...] = jnp.dot(la[i], kb[j], preferred_element_type=f32)


def tile_terms(i, j, same, ab, st, rb, cf):
    xi = jnp.where(same, 4, 0)
    rows = 16
    right = [jnp.broadcast_to(rb[j, q : q + 1, :], (rows, 128)) for q in range(4)]
    for c in range(128 // rows):
        sl = slice(rows * c, rows * c + rows)
        dx = ab[i, xi, sl, :] - right[0]
        dy = ab[i, 1, sl, :] - right[1]
        dz = ab[i, 2, sl, :] - right[2]
        rs = ab[i, 3, sl, :] + right[3]
        d2 = jnp.minimum(dx * dx + dy * dy + dz * dz, 1e37)
        inv = lax.rsqrt(d2)
        depth = jnp.maximum(rs - d2 * inv, 0.0)
        rc = depth * lax.rsqrt(jnp.maximum(depth * rs, 1e-35))
        ga = rc * inv
        gi = ga * inv
        al = ga * depth - gi * st[sl, 0:128]
        de = gi * st[sl, 128:256]
        for n, co in enumerate((al, rc, ga, de)):
            h = co.astype(bf16)
            cf[128 * n + rows * c : 128 * n + rows * c + rows, 0:128] = h
            cf[128 * n + rows * c : 128 * n + rows * c + rows, 128:256] = (
                co - h.astype(f32)
            ).astype(bf16)


def tile_sums(i, j, mult, wb, cf, acc):
    o = lax.dot_general(
        wb[j], cf[...], (((1,), (1,)), ((), ())), preferred_element_type=f32
    )
    o = (o[0:16] + o[16:32] + o[32:48]) * mult
    for q in range(4):
        at = pl.ds(pl.multiple_of(i * 16, 16) + 128 * q, 16)
        acc[at, :] = acc[at, :] + o[:, 128 * q : 128 * q + 128]


def tile_loop(start, stop, list_ref, ab, la, rb, kb, wb, cfs, sts, acc, base_j=0):
    def get(e):
        live = e < stop
        code = jnp.where(live, list_ref[0, e], 8 * base_j)
        often = jnp.where(live, list_ref[1, e], 0)
        return code & 7, (code >> 3) - base_j, often.astype(f32)

    trips = (stop - start + U - 1) // U
    for cf in cfs:
        cf[...] = jnp.zeros_like(cf)
    for n in range(U):
        i, j, _ = get(start + n)
        tile_dots(i, j, la, kb, sts[n])

    def body(t, prev):
        base = start + U * t
        cur = [get(base + n) for n in range(U)]
        for n in range(U):
            i, j, mult = prev[n]
            tile_sums(i, j, mult, wb, cfs[n], acc)
        for n in range(U):
            i, j, _ = cur[n]
            tile_terms(i, j, i == j + base_j, ab, sts[n], rb, cfs[n])
        for n in range(U):
            i, j, _ = get(base + U + n)
            tile_dots(i, j, la, kb, sts[n])
        return tuple(cur)

    none = (jnp.int32(0), jnp.int32(0), jnp.float32(0))
    prev = lax.fori_loop(0, trips, body, (none,) * U)
    for n in range(U):
        i, j, mult = prev[n]
        tile_sums(i, j, mult, wb, cfs[n], acc)


def prep_kernel(d, ab, la, rb, kb, wb, feat):
    left_prep(lambda c: d[c], ab, la, feat)
    right_prep(lambda c: d[c], NB, range(NB), rb, kb, wb, feat)


def own_kernel(list_ref, ab, la, rb, kb, wb, acc, *bufs):
    acc[...] = jnp.zeros_like(acc)
    tile_loop(jnp.int32(0), list_ref[2, 0], list_ref, ab, la, rb, kb, wb, bufs[:U], bufs[U:], acc)


def ghost_kernel(list_ref, d, ab, la, part, below, line, above, out, acc, rb, kb, wb, feat, *bufs):
    acc[...] = part[...]
    for ref, lo in ((below, 0), (line, 6), (above, 12)):
        right_prep(lambda c: ref[pl.ds(c, 6, stride=16), :], 6, range(lo, lo + 6), rb, kb, wb, feat)
    tile_loop(
        list_ref[2, 0], list_ref[3, 0], list_ref, ab, la, rb, kb, wb, bufs[:U], bufs[U:], acc, NB
    )
    finish(d, acc, out)


def finish(d, acc, out):
    need = (4, 10, 16, 4)
    a, b, g, e = (
        [acc[pl.ds(128 * q + r, NB, stride=16), :] for r in range(need[q])]
        for q in range(4)
    )
    x, v, u, rp = scaled(lambda c: d[c])
    uxg = cross(u, g[1:4])
    ux = cross(u, x)
    gux = cross(g[7:10], x)
    xv = cross(x, v)
    xgv = cross(x, g[4:7])
    gxv = cross(g[1:4], v)
    r = d[12]
    mass = (DENSITY * (4.0 / 3.0) * jnp.pi) * (r * r * r)
    inertia = 0.4 * mass * r * r
    half = 0.5 * jnp.sqrt(rp)
    to_acc = half / mass
    to_ang = half * r * DT / inertia
    for c in range(3):
        force = (
            x[c] * (a[0] - g[0])
            - (a[1 + c] - g[1 + c])
            - (v[c] * b[0] - b[4 + c])
            + (ux[c] * g[0] - uxg[c] + gux[c] - g[10 + c])
        )
        torque = (
            (xv[c] * g[0] - xgv[c] - gxv[c] + g[13 + c])
            - (u[c] * b[0] + b[7 + c])
            + (x[c] * e[0] - e[1 + c])
        )
        accel = force * to_acc
        if c == 2:
            accel = accel - 1.0
        out[c] = d[c]
        out[3 + c] = v[c] + (0.5 * DT) * (d[9 + c] + accel)
        out[6 + c] = d[6 + c] + torque * to_ang
        out[9 + c] = accel
    out[12] = r


VM = pl.BlockSpec(memory_space=pltpu.VMEM)
SM = pl.BlockSpec(memory_space=pltpu.SMEM)


def kernel_call(body, name, ins, outs, scratch=(), flags=None):
    args = [
        x if space == "hbm" else pltpu.with_memory_space_constraint(
            x, pltpu.SMEM if space == "smem" else pltpu.VMEM
        )
        for x, space in ins
    ]
    return pl.pallas_call(
        body,
        out_shape=outs,
        in_specs=[SM if space == "smem" else VM for _, space in ins],
        out_specs=tuple(VM for _ in outs),
        scratch_shapes=list(scratch),
        compiler_params=pltpu.CompilerParams(flags=flags, vmem_limit_bytes=16 << 20),
        name=name,
    )(*args)


def per_device(spheres, new_home, ghost_list, tile_pairs, tile_count):
    local = spheres.reshape(13, NB, 128)
    me = lax.axis_index("gx").astype(i32)[None]
    block = pltpu.VMEM((13, NB, 128), f32)
    bufs = kernel_call(
        pack_kernel,
        "pack",
        [(new_home, "smem"), (me, "smem"), (local, "hbm")],
        (block,) * 4,
        [pltpu.VMEM((4, 13, NB, 128), f32)],
    )
    came = [passed_along(bufs[k], "gx", k) for k in range(1, SPAN + 1)]
    (order,) = kernel_call(
        list_kernel,
        "tile_list",
        [(tile_count, "smem"), (tile_pairs[0].T, "hbm")],
        (jax.ShapeDtypeStruct((8, 256), i32),),
    )
    order, *came = lax.optimization_barrier((order, *came))
    drifted, lent = kernel_call(
        drift_kernel,
        "drift",
        [(ghost_list, "smem")] + [(x, "vmem") for x in (bufs[0], *came)],
        (block, pltpu.VMEM((32, 128), f32)),
    )
    behind = passed_along(lent, "gx", 1)
    front = passed_along(lent, "gx", -1)
    feat = pltpu.VMEM((512, 128), f32)
    ab, la, rb, kb, wb = kernel_call(
        prep_kernel,
        "prep",
        [(drifted, "vmem")],
        (
            pltpu.VMEM((NB, 5, 128, 128), f32),
            pltpu.VMEM((NB, 128, 128), bf16),
            pltpu.VMEM((NB, 8, 128), f32),
            pltpu.VMEM((NB, 128, 256), bf16),
            pltpu.VMEM((NB, 48, 256), bf16),
        ),
        [feat],
    )
    rb, behind, front = lax.optimization_barrier((rb, behind, front))
    line = jnp.concatenate([behind, lent, front], 0)
    below = passed_along(line, "gy", 1)
    above = passed_along(line, "gy", -1)
    work = [pltpu.VMEM((512, 256), bf16)] * U + [pltpu.VMEM((128, 256), f32)] * U
    sums = pltpu.VMEM((4 * NB * 16, 128), f32)
    (part,) = kernel_call(
        own_kernel,
        "own",
        [(order, "smem")] + [(x, "vmem") for x in (ab, la, rb, kb, wb)],
        (sums,),
        work,
        FLAGS,
    )
    (out,) = kernel_call(
        ghost_kernel,
        "ghost",
        [(order, "smem")] + [(x, "vmem") for x in (drifted, ab, la, part, below, line, above)],
        (jax.ShapeDtypeStruct((13, NB, 128), f32),),
        [
            sums,
            pltpu.VMEM((18, 8, 128), f32),
            pltpu.VMEM((18, 128, 256), bf16),
            pltpu.VMEM((18, 48, 256), bf16),
            feat,
        ]
        + work,
        FLAGS,
    )
    return out[:, None]


def solution(mesh):
    in_specs = (
        P(None, "gy", "gx", None),
        P("gy", "gx"),
        P("gy", "gx"),
        P("gy", "gx", None),
        P("gy", "gx"),
    )
    return jax.shard_map(
        per_device,
        mesh=mesh,
        in_specs=in_specs,
        out_specs=P(None, "gy", "gx", None),
        check_vma=False,
    )
```

```python
import jax
import jax.numpy as jnp
from jax import lax
from jax.experimental import pallas as pl
from jax.experimental.pallas import tpu as pltpu
from jax.sharding import PartitionSpec as P

SPAN = 3
DT = 0.01
DENSITY = 240.0
SC = 20.0
NB = 8
NP = 26
NT = NB * NP
U = 8
LAG = 2
FLAGS = None

f32 = jnp.float32
bf16 = jnp.bfloat16
i32 = jnp.int32


def passed_along(x, axis, by):
    peers = lax.axis_size(axis)
    return lax.ppermute(x, axis, [(i, (i + by) % peers) for i in range(peers)])


def pack_kernel(home_ref, me_ref, x_ref, b0, b1, b2, b3, buf):
    buf[...] = jnp.zeros_like(buf)
    for b in range(NB):
        home = home_ref[0, b]
        ahead = ((home >> 3) - me_ref[0]) & 31
        buf[ahead, :, pl.ds(home & 7, 1), :] = x_ref[:, b : b + 1, :]
    for k, out in enumerate((b0, b1, b2, b3)):
        out[...] = buf[k]


def list_kernel(count_ref, pairs_ref, out):
    lane = lax.broadcasted_iota(i32, (1, 256), 1)
    code = jnp.where(lane < count_ref[0, 0], pairs_ref[1:2, :] * NB + pairs_ref[0:1, :], 255)
    rows = 224
    c = lax.broadcasted_iota(i32, (rows, 256), 0)
    hit = jnp.where(code == c, 1.0, 0.0).astype(bf16)
    often = jnp.dot(hit, jnp.ones((256, 128), bf16), preferred_element_type=f32)
    ci = lax.broadcasted_iota(i32, (rows, 128), 0)
    there = (often > 0.5) & (ci < NT)
    r = lax.broadcasted_iota(i32, (rows, rows), 0)
    q = lax.broadcasted_iota(i32, (rows, rows), 1)
    rank = jnp.dot(
        jnp.where(q < r, 1.0, 0.0).astype(bf16),
        jnp.where(there, 1.0, 0.0).astype(bf16),
        preferred_element_type=f32,
    )
    cf = ci.astype(f32)
    for half in range(2):
        e = lax.broadcasted_iota(i32, (rows, 128), 1).astype(f32) + 128.0 * half
        pick = there & (rank == e)
        sl = slice(128 * half, 128 * half + 128)
        out[0:1, sl] = jnp.sum(jnp.where(pick, cf, 0.0), 0, keepdims=True).astype(i32)
        out[1:2, sl] = jnp.sum(jnp.where(pick, often, 0.0), 0, keepdims=True).astype(i32)
        out[2:3, sl] = rank[64:65].astype(i32)
        out[3:4, sl] = rank[NT : NT + 1].astype(i32)


def drift_kernel(lent_ref, a0, a1, a2, a3, drifted, lent):
    x = a0[...] + a1[...] + a2[...] + a3[...]
    drifted[3:13] = x[3:13]
    drifted[0:3] = x[0:3] + DT * x[3:6] + (0.5 * DT * DT) * x[9:12]
    for q in range(2):
        slot = lent_ref[0, q]
        for c in range(13):
            lent[16 * q + c : 16 * q + c + 1, :] = drifted[c, pl.ds(slot, 1), :]
        lent[16 * q + 13 : 16 * q + 16, :] = jnp.zeros((3, 128), f32)


def split3(f):
    h = f.astype(bf16)
    r = f - h.astype(f32)
    m = r.astype(bf16)
    return h, m, (r - m.astype(f32)).astype(bf16)


def cross(a, b):
    return [
        a[1] * b[2] - a[2] * b[1],
        a[2] * b[0] - a[0] * b[2],
        a[0] * b[1] - a[1] * b[0],
    ]


def dot3(a, b):
    return a[0] * b[0] + a[1] * b[1] + a[2] * b[2]


def scaled(get):
    x = [get(c) * SC for c in range(3)]
    v = [get(3 + c) for c in range(3)]
    r = get(12)
    u = [r * get(6 + c) for c in range(3)]
    return x, v, u, r * SC


def left_prep(get, ab, la, feat):
    x, v, u, rp = scaled(get)
    zero = jnp.zeros_like(rp)
    rows = x + v + u + [dot3(x, v), dot3(x, u), jnp.ones_like(rp), rp, zero, zero, zero]
    for n, q in enumerate(rows):
        feat[pl.ds(n, NB, stride=16), :] = q
    a = lax.broadcasted_iota(i32, (128, 128), 0)
    b = lax.broadcasted_iota(i32, (128, 128), 1)
    for i in range(NB):
        f = feat[16 * i : 16 * i + 16, :]
        h, m, l = (p.astype(f32) for p in split3(f))
        t = jnp.concatenate([h, h, m, m, h, l, f, jnp.zeros((16, 128), f32)], 0).T
        la[i] = jnp.where(b < 96, t, 0.0).astype(bf16)
        for n, c in enumerate((96, 97, 98, 108)):
            ab[i, n] = jnp.broadcast_to(t[:, c : c + 1], (128, 128))
        ab[i, 4] = jnp.where(a == b, 1e15, jnp.broadcast_to(t[:, 96:97], (128, 128)))


def right_prep(get, nb, at, rb, kb, wb, feat):
    x, v, u, rp = scaled(get)
    one = jnp.ones_like(rp)
    zero = jnp.zeros_like(rp)
    neg = lambda a: [-q for q in a]
    sb = jnp.sqrt(rp)
    s = neg(v) + neg(x) + [zero] * 3 + [one, zero, dot3(x, v)]
    t = u + [zero] * 3 + neg(x) + [zero, one, -dot3(x, u)]
    w = [sb * q for q in [one] + x + v + u + cross(u, x) + cross(x, v)]
    for k, rows in enumerate((s, t, w, x + [rp])):
        for n in range(16 if k < 3 else 4):
            feat[pl.ds(128 * k + n, nb, stride=16), :] = rows[n] if n < len(rows) else zero
    for p in range(nb):
        j = at[p]
        fs, ft, fw = (feat[128 * k + 16 * p : 128 * k + 16 * p + 16, :] for k in range(3))
        rb[j] = feat[384 + 16 * p : 384 + 16 * p + 8, :]
        sh, sm, sl = split3(fs)
        th, tm, tl = split3(ft)
        for n, (p0, p1) in enumerate(
            ((sh, th), (sm, tm), (sh, th), (sm, tm), (sl, tl), (sh, th))
        ):
            kb[j, 16 * n : 16 * n + 16, 0:128] = p0
            kb[j, 16 * n : 16 * n + 16, 128:256] = p1
        kb[j, 96:128, :] = jnp.zeros((32, 256), bf16)
        for n, p0 in enumerate(split3(fw)):
            wb[j, 16 * n : 16 * n + 16, 0:128] = p0
            wb[j, 16 * n : 16 * n + 16, 128:256] = p0


def tile_dots(i, j, la, kb, st):
    st[...] = jnp.dot(la[i], kb[j], preferred_element_type=f32)


def tile_terms(i, j, same, ab, st, rb, cf):
    xi = jnp.where(same, 4, 0)
    rows = 16
    right = [jnp.broadcast_to(rb[j, q : q + 1, :], (rows, 128)) for q in range(4)]
    for c in range(128 // rows):
        sl = slice(rows * c, rows * c + rows)
        dx = ab[i, xi, sl, :] - right[0]
        dy = ab[i, 1, sl, :] - right[1]
        dz = ab[i, 2, sl, :] - right[2]
        rs = ab[i, 3, sl, :] + right[3]
        d2 = jnp.minimum(dx * dx + dy * dy + dz * dz, 1e37)
        inv = lax.rsqrt(d2)
        depth = jnp.maximum(rs - d2 * inv, 0.0)
        rc = depth * lax.rsqrt(jnp.maximum(depth * rs, 1e-35))
        ga = rc * inv
        gi = ga * inv
        al = ga * depth - gi * st[sl, 0:128]
        de = gi * st[sl, 128:256]
        for n, co in enumerate((al, rc, ga, de)):
            h = co.astype(bf16)
            at = 128 * n + rows * c
            cf[at : at + rows, :] = h
            cf[512 + at : 512 + at + rows, :] = (co - h.astype(f32)).astype(bf16)


def tile_sums(i, j, mult, wb, cf, acc):
    both = jnp.concatenate([cf[0:512, :], cf[512:1024, :]], 1)
    o = lax.dot_general(wb[j], both, (((1,), (1,)), ((), ())), preferred_element_type=f32)
    o = (o[0:16] + o[16:32] + o[32:48]) * mult
    for q in range(4):
        at = pl.ds(pl.multiple_of(i * 16, 16) + 128 * q, 16)
        acc[at, :] = acc[at, :] + o[:, 128 * q : 128 * q + 128]


def tile_loop(start, stop, list_ref, ab, la, rb, kb, wb, cfs, sts, acc, base_j=0):
    def get(e):
        live = e < stop
        code = jnp.where(live, list_ref[0, e], 8 * base_j)
        often = jnp.where(live, list_ref[1, e], 0)
        return code & 7, (code >> 3) - base_j, often.astype(f32)

    trips = (stop - start + U - 1) // U
    for n in range(U - LAG, U):
        cfs[n][...] = jnp.zeros_like(cfs[n])
    for n in range(U):
        i, j, _ = get(start + n)
        tile_dots(i, j, la, kb, sts[n])

    def body(t, late):
        base = start + U * t
        late = list(late)
        for n in range(U):
            i, j, mult = get(base + n)
            tile_terms(i, j, i == j + base_j, ab, sts[n], rb, cfs[n])
            late.append((i, j, mult))
            i, j, mult = late.pop(0)
            tile_sums(i, j, mult, wb, cfs[(n - LAG) % U], acc)
            i, j, _ = get(base + U + n)
            tile_dots(i, j, la, kb, sts[n])
        return tuple(late)

    none = (jnp.int32(0), jnp.int32(0), jnp.float32(0))
    late = lax.fori_loop(0, trips, body, (none,) * LAG)
    for n, (i, j, mult) in enumerate(late):
        tile_sums(i, j, mult, wb, cfs[U - LAG + n], acc)


def prep_kernel(d, ab, la, rb, kb, wb, feat):
    left_prep(lambda c: d[c], ab, la, feat)
    right_prep(lambda c: d[c], NB, range(NB), rb, kb, wb, feat)


def own_kernel(list_ref, ab, la, rb, kb, wb, acc, *bufs):
    acc[...] = jnp.zeros_like(acc)
    tile_loop(jnp.int32(0), list_ref[2, 0], list_ref, ab, la, rb, kb, wb, bufs[:U], bufs[U:], acc)


def ghost_kernel(list_ref, d, ab, la, part, below, line, above, out, acc, rb, kb, wb, feat, *bufs):
    acc[...] = part[...]
    for ref, lo in ((below, 0), (line, 6), (above, 12)):
        right_prep(lambda c: ref[pl.ds(c, 6, stride=16), :], 6, range(lo, lo + 6), rb, kb, wb, feat)
    tile_loop(
        list_ref[2, 0], list_ref[3, 0], list_ref, ab, la, rb, kb, wb, bufs[:U], bufs[U:], acc, NB
    )
    finish(d, acc, out)


def finish(d, acc, out):
    need = (4, 10, 16, 4)
    a, b, g, e = (
        [acc[pl.ds(128 * q + r, NB, stride=16), :] for r in range(need[q])]
        for q in range(4)
    )
    x, v, u, rp = scaled(lambda c: d[c])
    uxg = cross(u, g[1:4])
    ux = cross(u, x)
    gux = cross(g[7:10], x)
    xv = cross(x, v)
    xgv = cross(x, g[4:7])
    gxv = cross(g[1:4], v)
    r = d[12]
    mass = (DENSITY * (4.0 / 3.0) * jnp.pi) * (r * r * r)
    inertia = 0.4 * mass * r * r
    half = 0.5 * jnp.sqrt(rp)
    to_acc = half / mass
    to_ang = half * r * DT / inertia
    for c in range(3):
        force = (
            x[c] * (a[0] - g[0])
            - (a[1 + c] - g[1 + c])
            - (v[c] * b[0] - b[4 + c])
            + (ux[c] * g[0] - uxg[c] + gux[c] - g[10 + c])
        )
        torque = (
            (xv[c] * g[0] - xgv[c] - gxv[c] + g[13 + c])
            - (u[c] * b[0] + b[7 + c])
            + (x[c] * e[0] - e[1 + c])
        )
        accel = force * to_acc
        if c == 2:
            accel = accel - 1.0
        out[c] = d[c]
        out[3 + c] = v[c] + (0.5 * DT) * (d[9 + c] + accel)
        out[6 + c] = d[6 + c] + torque * to_ang
        out[9 + c] = accel
    out[12] = r


VM = pl.BlockSpec(memory_space=pltpu.VMEM)
SM = pl.BlockSpec(memory_space=pltpu.SMEM)


def kernel_call(body, name, ins, outs, scratch=(), flags=None):
    args = [
        x if space == "hbm" else pltpu.with_memory_space_constraint(
            x, pltpu.SMEM if space == "smem" else pltpu.VMEM
        )
        for x, space in ins
    ]
    return pl.pallas_call(
        body,
        out_shape=outs,
        in_specs=[SM if space == "smem" else VM for _, space in ins],
        out_specs=tuple(VM for _ in outs),
        scratch_shapes=list(scratch),
        compiler_params=pltpu.CompilerParams(flags=flags, vmem_limit_bytes=16 << 20),
        name=name,
    )(*args)


def prep_call(drifted):
    return kernel_call(
        prep_kernel,
        "prep",
        [(drifted, "vmem")],
        (
            pltpu.VMEM((NB, 5, 128, 128), f32),
            pltpu.VMEM((NB, 128, 128), bf16),
            pltpu.VMEM((NB, 8, 128), f32),
            pltpu.VMEM((NB, 128, 256), bf16),
            pltpu.VMEM((NB, 48, 256), bf16),
        ),
        [pltpu.VMEM((512, 128), f32)],
    )


def tiles_call(order, drifted, made, below, line, above):
    ab, la, rb, kb, wb = made
    feat = pltpu.VMEM((512, 128), f32)
    work = [pltpu.VMEM((1024, 128), bf16)] * U + [pltpu.VMEM((128, 256), f32)] * U
    sums = pltpu.VMEM((4 * NB * 16, 128), f32)
    (part,) = kernel_call(
        own_kernel,
        "own",
        [(order, "smem")] + [(x, "vmem") for x in (ab, la, rb, kb, wb)],
        (sums,),
        work,
        FLAGS,
    )
    (out,) = kernel_call(
        ghost_kernel,
        "ghost",
        [(order, "smem")] + [(x, "vmem") for x in (drifted, ab, la, part, below, line, above)],
        (jax.ShapeDtypeStruct((13, NB, 128), f32),),
        [
            sums,
            pltpu.VMEM((18, 8, 128), f32),
            pltpu.VMEM((18, 128, 256), bf16),
            pltpu.VMEM((18, 48, 256), bf16),
            feat,
        ]
        + work,
        FLAGS,
    )
    return out


def compute(order, drifted, below, line, above):
    return tiles_call(order, drifted, prep_call(drifted), below, line, above)


def per_device(spheres, new_home, ghost_list, tile_pairs, tile_count):
    local = spheres.reshape(13, NB, 128)
    me = lax.axis_index("gx").astype(i32)[None]
    block = pltpu.VMEM((13, NB, 128), f32)
    bufs = kernel_call(
        pack_kernel,
        "pack",
        [(new_home, "smem"), (me, "smem"), (local, "hbm")],
        (block,) * 4,
        [pltpu.VMEM((4, 13, NB, 128), f32)],
    )
    came = [passed_along(bufs[k], "gx", k) for k in range(1, SPAN + 1)]
    (order,) = kernel_call(
        list_kernel,
        "tile_list",
        [(tile_count, "smem"), (tile_pairs[0].T, "hbm")],
        (jax.ShapeDtypeStruct((8, 256), i32),),
    )
    order, *came = lax.optimization_barrier((order, *came))
    drifted, lent = kernel_call(
        drift_kernel,
        "drift",
        [(ghost_list, "smem")] + [(x, "vmem") for x in (bufs[0], *came)],
        (block, pltpu.VMEM((32, 128), f32)),
    )
    behind = passed_along(lent, "gx", 1)
    front = passed_along(lent, "gx", -1)
    made = prep_call(drifted)
    first, behind, front = lax.optimization_barrier((made[2], behind, front))
    made = (*made[:2], first, *made[3:])
    line = jnp.concatenate([behind, lent, front], 0)
    below = passed_along(line, "gy", 1)
    above = passed_along(line, "gy", -1)
    return tiles_call(order, drifted, made, below, line, above)[:, None]


def solution(mesh):
    in_specs = (
        P(None, "gy", "gx", None),
        P("gy", "gx"),
        P("gy", "gx"),
        P("gy", "gx", None),
        P("gy", "gx"),
    )
    return jax.shard_map(
        per_device,
        mesh=mesh,
        in_specs=in_specs,
        out_specs=P(None, "gy", "gx", None),
        check_vma=False,
    )
```

```python
import jax
import jax.numpy as jnp
from jax import lax
from jax.experimental import pallas as pl
from jax.experimental.pallas import tpu as pltpu
from jax.sharding import PartitionSpec as P

DT = 0.01
DENSITY = 240.0
SC = 20.0
NB = 8
NP = 26
NT = NB * NP
U = 8
FIRST = 16
LAG = 2
FLAGS = None

f32 = jnp.float32
bf16 = jnp.bfloat16
i32 = jnp.int32


def passed_along(x, axis, by):
    peers = lax.axis_size(axis)
    return lax.ppermute(x, axis, [(i, (i + by) % peers) for i in range(peers)])


def embed_kernel(home_ref, x_ref, out):
    out[0:13] = x_ref[...]
    row = lax.broadcasted_iota(i32, (NB, 128), 0)
    home = jnp.zeros((NB, 128), i32)
    for b in range(NB):
        home = jnp.where(row == b, home_ref[0, b], home)
    out[13] = home.astype(f32)


def sort_kernel(mine, past, keep, onward):
    me = lax.axis_index("gx").astype(i32)
    row = lax.broadcasted_iota(i32, (NB, 128), 0)
    here = (me * NB + row).astype(f32)
    there = (((me + 2) & 31) * NB + row).astype(f32)
    held = []
    for ref in (mine, past):
        for t in range(NB):
            home = ref[13] if t == 0 else pltpu.roll(ref[13], t, 0)
            held.append((ref, t, home == here, home == there))
    for c in range(13):
        stay = jnp.zeros((NB, 128), f32)
        go = jnp.zeros((NB, 128), f32)
        for ref, t, is_here, is_there in held:
            x = ref[c] if t == 0 else pltpu.roll(ref[c], t, 0)
            stay = jnp.where(is_here, x, stay)
            go = jnp.where(is_there, x, go)
        keep[c] = stay
        onward[c] = go


def list_kernel(count_ref, lent_ref, pairs_ref, out_ref, out, sem):
    lane = lax.broadcasted_iota(i32, (1, 256), 1)
    code = jnp.where(lane < count_ref[0, 0], pairs_ref[1:2, :] * NB + pairs_ref[0:1, :], 255)
    rows = 224
    c = lax.broadcasted_iota(i32, (rows, 256), 0)
    hit = jnp.where(code == c, 1.0, 0.0).astype(bf16)
    often = jnp.dot(hit, jnp.ones((256, 128), bf16), preferred_element_type=f32)
    ci = lax.broadcasted_iota(i32, (rows, 128), 0)
    there = (often > 0.5) & (ci < NT)
    r = lax.broadcasted_iota(i32, (rows, rows), 0)
    q = lax.broadcasted_iota(i32, (rows, rows), 1)
    rank = jnp.dot(
        jnp.where(q < r, 1.0, 0.0).astype(bf16),
        jnp.where(there, 1.0, 0.0).astype(bf16),
        preferred_element_type=f32,
    )
    cf = ci.astype(f32)
    for half in range(2):
        e = lax.broadcasted_iota(i32, (rows, 128), 1).astype(f32) + 128.0 * half
        pick = there & (rank == e)
        sl = slice(128 * half, 128 * half + 128)
        out[0:1, sl] = jnp.sum(jnp.where(pick, cf, 0.0), 0, keepdims=True).astype(i32)
        out[1:2, sl] = jnp.sum(jnp.where(pick, often, 0.0), 0, keepdims=True).astype(i32)
        out[2:3, sl] = rank[64:65].astype(i32)
        out[3:4, sl] = rank[NT : NT + 1].astype(i32)
    copy = pltpu.make_async_copy(out, out_ref, sem)
    copy.start()
    copy.wait()
    for q in range(2):
        out_ref[4, q] = lent_ref[0, q]


def drift_kernel(list_ref, keep, came, drifted, lent):
    x = keep[...] + came[...]
    drifted[3:13] = x[3:13]
    drifted[0:3] = x[0:3] + DT * x[3:6] + (0.5 * DT * DT) * x[9:12]
    for q in range(2):
        slot = list_ref[4, q]
        for c in range(13):
            lent[16 * q + c : 16 * q + c + 1, :] = drifted[c, pl.ds(slot, 1), :]
        lent[16 * q + 13 : 16 * q + 16, :] = jnp.zeros((3, 128), f32)


def split3(f):
    h = f.astype(bf16)
    r = f - h.astype(f32)
    m = r.astype(bf16)
    return h, m, (r - m.astype(f32)).astype(bf16)


def cross(a, b):
    return [
        a[1] * b[2] - a[2] * b[1],
        a[2] * b[0] - a[0] * b[2],
        a[0] * b[1] - a[1] * b[0],
    ]


def dot3(a, b):
    return a[0] * b[0] + a[1] * b[1] + a[2] * b[2]


def scaled(get):
    x = [get(c) * SC for c in range(3)]
    v = [get(3 + c) for c in range(3)]
    r = get(12)
    u = [r * get(6 + c) for c in range(3)]
    return x, v, u, r * SC


def left_prep(get, ab, la, feat):
    x, v, u, rp = scaled(get)
    zero = jnp.zeros_like(rp)
    rows = x + v + u + [dot3(x, v), dot3(x, u), jnp.ones_like(rp), rp, zero, zero, zero]
    for n, q in enumerate(rows):
        feat[pl.ds(n, NB, stride=16), :] = q
    a = lax.broadcasted_iota(i32, (128, 128), 0)
    b = lax.broadcasted_iota(i32, (128, 128), 1)
    for i in range(NB):
        f = feat[16 * i : 16 * i + 16, :]
        h, m, l = (p.astype(f32) for p in split3(f))
        t = jnp.concatenate([h, h, m, m, h, l, f, jnp.zeros((16, 128), f32)], 0).T
        la[i] = jnp.where(b < 96, t, 0.0).astype(bf16)
        for n, c in enumerate((96, 97, 98, 108)):
            ab[i, n] = jnp.broadcast_to(t[:, c : c + 1], (128, 128))
        ab[i, 4] = jnp.where(a == b, 1e15, jnp.broadcast_to(t[:, 96:97], (128, 128)))


def right_prep(get, nb, at, rb, kb, wb, feat):
    x, v, u, rp = scaled(get)
    one = jnp.ones_like(rp)
    zero = jnp.zeros_like(rp)
    neg = lambda a: [-q for q in a]
    sb = jnp.sqrt(rp)
    s = neg(v) + neg(x) + [zero] * 3 + [one, zero, dot3(x, v)]
    t = u + [zero] * 3 + neg(x) + [zero, one, -dot3(x, u)]
    w = [sb * q for q in [one] + x + v + u + cross(u, x) + cross(x, v)]
    for k, rows in enumerate((s, t, w, x + [rp])):
        for n in range(16 if k < 3 else 4):
            feat[pl.ds(128 * k + n, nb, stride=16), :] = rows[n] if n < len(rows) else zero
    for p in range(nb):
        j = at[p]
        fs, ft, fw = (feat[128 * k + 16 * p : 128 * k + 16 * p + 16, :] for k in range(3))
        rb[j] = feat[384 + 16 * p : 384 + 16 * p + 8, :]
        sh, sm, sl = split3(fs)
        th, tm, tl = split3(ft)
        for n, (p0, p1) in enumerate(
            ((sh, th), (sm, tm), (sh, th), (sm, tm), (sl, tl), (sh, th))
        ):
            kb[j, 16 * n : 16 * n + 16, 0:128] = p0
            kb[j, 16 * n : 16 * n + 16, 128:256] = p1
        kb[j, 96:128, :] = jnp.zeros((32, 256), bf16)
        for n, p0 in enumerate(split3(fw)):
            wb[j, 16 * n : 16 * n + 16, 0:128] = p0
            wb[j, 16 * n : 16 * n + 16, 128:256] = p0


def tile_dots(i, j, la, kb, st):
    st[...] = jnp.dot(la[i], kb[j], preferred_element_type=f32)


def tile_terms(i, j, same, ab, st, rb, cf):
    xi = jnp.where(same, 4, 0)
    rows = 16
    right = [jnp.broadcast_to(rb[j, q : q + 1, :], (rows, 128)) for q in range(4)]
    for c in range(128 // rows):
        sl = slice(rows * c, rows * c + rows)
        dx = ab[i, xi, sl, :] - right[0]
        dy = ab[i, 1, sl, :] - right[1]
        dz = ab[i, 2, sl, :] - right[2]
        rs = ab[i, 3, sl, :] + right[3]
        d2 = jnp.minimum(dx * dx + dy * dy + dz * dz, 1e37)
        inv = lax.rsqrt(d2)
        depth = jnp.maximum(rs - d2 * inv, 0.0)
        rc = depth * lax.rsqrt(jnp.maximum(depth * rs, 1e-35))
        ga = rc * inv
        gi = ga * inv
        al = ga * depth - gi * st[sl, 0:128]
        de = gi * st[sl, 128:256]
        for n, co in enumerate((al, rc, ga, de)):
            h = co.astype(bf16)
            at = 128 * n + rows * c
            cf[at : at + rows, :] = h
            cf[512 + at : 512 + at + rows, :] = (co - h.astype(f32)).astype(bf16)


def tile_sums(i, j, mult, wb, cf, acc):
    both = jnp.concatenate([cf[0:512, :], cf[512:1024, :]], 1)
    o = lax.dot_general(wb[j], both, (((1,), (1,)), ((), ())), preferred_element_type=f32)
    o = (o[0:16] + o[16:32] + o[32:48]) * mult
    for q in range(4):
        at = pl.ds(pl.multiple_of(i * 16, 16) + 128 * q, 16)
        acc[at, :] = acc[at, :] + o[:, 128 * q : 128 * q + 128]


def tile_loop(start, stop, list_ref, ab, la, rb, kb, wb, cfs, sts, acc, base_j=0):
    def get(e):
        live = e < stop
        code = jnp.where(live, list_ref[0, e], 8 * base_j)
        often = jnp.where(live, list_ref[1, e], 0)
        return code & 7, (code >> 3) - base_j, often.astype(f32)

    trips = (stop - start + U - 1) // U
    for n in range(U - LAG, U):
        cfs[n][...] = jnp.zeros_like(cfs[n])
    for n in range(U):
        i, j, _ = get(start + n)
        tile_dots(i, j, la, kb, sts[n])

    def body(t, late):
        base = start + U * t
        late = list(late)
        for n in range(U):
            i, j, mult = get(base + n)
            tile_terms(i, j, i == j + base_j, ab, sts[n], rb, cfs[n])
            late.append((i, j, mult))
            i, j, mult = late.pop(0)
            tile_sums(i, j, mult, wb, cfs[(n - LAG) % U], acc)
            i, j, _ = get(base + U + n)
            tile_dots(i, j, la, kb, sts[n])
        return tuple(late)

    none = (jnp.int32(0), jnp.int32(0), jnp.float32(0))
    late = lax.fori_loop(0, trips, body, (none,) * LAG)
    for n, (i, j, mult) in enumerate(late):
        tile_sums(i, j, mult, wb, cfs[U - LAG + n], acc)


def first_kernel(list_ref, d, ab, la, rb, kb, wb, acc, feat, *bufs):
    left_prep(lambda c: d[c], ab, la, feat)
    right_prep(lambda c: d[c], NB, range(NB), rb, kb, wb, feat)
    acc[...] = jnp.zeros_like(acc)
    stop = jnp.minimum(list_ref[2, 0], FIRST)
    tile_loop(jnp.int32(0), stop, list_ref, ab, la, rb, kb, wb, bufs[:U], bufs[U:], acc)


def own_kernel(list_ref, ab, la, rb, kb, wb, part, acc, *bufs):
    acc[...] = part[...]
    start = jnp.minimum(list_ref[2, 0], FIRST)
    tile_loop(start, list_ref[2, 0], list_ref, ab, la, rb, kb, wb, bufs[:U], bufs[U:], acc)


def ghost_kernel(list_ref, d, ab, la, part, below, line, above, out, acc, rb, kb, wb, feat, *bufs):
    acc[...] = part[...]
    for ref, lo in ((below, 0), (line, 6), (above, 12)):
        right_prep(lambda c: ref[pl.ds(c, 6, stride=16), :], 6, range(lo, lo + 6), rb, kb, wb, feat)
    tile_loop(
        list_ref[2, 0], list_ref[3, 0], list_ref, ab, la, rb, kb, wb, bufs[:U], bufs[U:], acc, NB
    )
    finish(d, acc, out)


def finish(d, acc, out):
    need = (4, 10, 16, 4)
    a, b, g, e = (
        [acc[pl.ds(128 * q + r, NB, stride=16), :] for r in range(need[q])]
        for q in range(4)
    )
    x, v, u, rp = scaled(lambda c: d[c])
    uxg = cross(u, g[1:4])
    ux = cross(u, x)
    gux = cross(g[7:10], x)
    xv = cross(x, v)
    xgv = cross(x, g[4:7])
    gxv = cross(g[1:4], v)
    r = d[12]
    mass = (DENSITY * (4.0 / 3.0) * jnp.pi) * (r * r * r)
    inertia = 0.4 * mass * r * r
    half = 0.5 * jnp.sqrt(rp)
    to_acc = half / mass
    to_ang = half * r * DT / inertia
    for c in range(3):
        force = (
            x[c] * (a[0] - g[0])
            - (a[1 + c] - g[1 + c])
            - (v[c] * b[0] - b[4 + c])
            + (ux[c] * g[0] - uxg[c] + gux[c] - g[10 + c])
        )
        torque = (
            (xv[c] * g[0] - xgv[c] - gxv[c] + g[13 + c])
            - (u[c] * b[0] + b[7 + c])
            + (x[c] * e[0] - e[1 + c])
        )
        accel = force * to_acc
        if c == 2:
            accel = accel - 1.0
        out[c] = d[c]
        out[3 + c] = v[c] + (0.5 * DT) * (d[9 + c] + accel)
        out[6 + c] = d[6 + c] + torque * to_ang
        out[9 + c] = accel
    out[12] = r


VM = pl.BlockSpec(memory_space=pltpu.VMEM)
SM = pl.BlockSpec(memory_space=pltpu.SMEM)


def kernel_call(body, name, ins, outs, scratch=(), flags=None):
    kinds = {"smem": pltpu.SMEM, "vmem": pltpu.VMEM, "sfar": pltpu.HBM, "hbm": pltpu.HBM}
    args = [
        pltpu.with_memory_space_constraint(x, kinds[space]) if space in kinds else x
        for x, space in ins
    ]
    return pl.pallas_call(
        body,
        out_shape=outs,
        in_specs=[SM if space in ("smem", "sfar", "scalar") else VM for _, space in ins],
        out_specs=tuple(
            SM if getattr(o, "memory_space", None) == pltpu.SMEM else VM for o in outs
        ),
        scratch_shapes=list(scratch),
        compiler_params=pltpu.CompilerParams(flags=flags, vmem_limit_bytes=16 << 20),
        name=name,
    )(*args)


WORK = [pltpu.VMEM((1024, 128), bf16)] * U + [pltpu.VMEM((128, 256), f32)] * U
FEAT = pltpu.VMEM((512, 128), f32)
SUMS = pltpu.VMEM((4 * NB * 16, 128), f32)


def first_call(order, drifted):
    return kernel_call(
        first_kernel,
        "first",
        [(order, "smem"), (drifted, "vmem")],
        (
            pltpu.VMEM((NB, 5, 128, 128), f32),
            pltpu.VMEM((NB, 128, 128), bf16),
            pltpu.VMEM((NB, 8, 128), f32),
            pltpu.VMEM((NB, 128, 256), bf16),
            pltpu.VMEM((NB, 48, 256), bf16),
            SUMS,
        ),
        [FEAT] + WORK,
        FLAGS,
    )


def tiles_call(order, drifted, made, below, line, above):
    ab, la, rb, kb, wb, part = made
    (part,) = kernel_call(
        own_kernel,
        "own",
        [(order, "smem")] + [(x, "vmem") for x in (ab, la, rb, kb, wb, part)],
        (SUMS,),
        WORK,
        FLAGS,
    )
    (out,) = kernel_call(
        ghost_kernel,
        "ghost",
        [(order, "smem")] + [(x, "vmem") for x in (drifted, ab, la, part, below, line, above)],
        (jax.ShapeDtypeStruct((13, NB, 128), f32),),
        [
            SUMS,
            pltpu.VMEM((18, 8, 128), f32),
            pltpu.VMEM((18, 128, 256), bf16),
            pltpu.VMEM((18, 48, 256), bf16),
            FEAT,
        ]
        + WORK,
        FLAGS,
    )
    return out


def compute(order, drifted, below, line, above):
    return tiles_call(order, drifted, first_call(order, drifted), below, line, above)


def per_device(spheres, new_home, ghost_list, tile_pairs, tile_count):
    block = pltpu.VMEM((13, NB, 128), f32)
    (mine,) = kernel_call(
        embed_kernel,
        "embed",
        [(new_home, "sfar"), (spheres.reshape(13, NB, 128), "hbm")],
        (pltpu.VMEM((14, NB, 128), f32),),
    )
    past = passed_along(mine, "gx", 1)
    keep, onward = kernel_call(
        sort_kernel, "sort", [(mine, "vmem"), (past, "vmem")], (block, block)
    )
    came = passed_along(onward, "gx", 2)
    (order,) = kernel_call(
        list_kernel,
        "tile_list",
        [(tile_count, "scalar"), (ghost_list, "sfar"), (tile_pairs[0].T, "hbm")],
        (pltpu.SMEM((8, 256), i32),),
        [pltpu.VMEM((8, 256), i32), pltpu.SemaphoreType.DMA(())],
    )
    order, came = lax.optimization_barrier((order, came))
    drifted, lent = kernel_call(
        drift_kernel,
        "drift",
        [(order, "smem"), (keep, "vmem"), (came, "vmem")],
        (block, pltpu.VMEM((32, 128), f32)),
    )
    behind = passed_along(lent, "gx", 1)
    front = passed_along(lent, "gx", -1)
    *made, part = first_call(order, drifted)
    part, behind, front = lax.optimization_barrier((part, behind, front))
    made.append(part)
    line = jnp.concatenate([behind, lent, front], 0)
    below = passed_along(line, "gy", 1)
    above = passed_along(line, "gy", -1)
    return tiles_call(order, drifted, made, below, line, above)[:, None]


def solution(mesh):
    in_specs = (
        P(None, "gy", "gx", None),
        P("gy", "gx"),
        P("gy", "gx"),
        P("gy", "gx", None),
        P("gy", "gx"),
    )
    return jax.shard_map(
        per_device,
        mesh=mesh,
        in_specs=in_specs,
        out_specs=P(None, "gy", "gx", None),
        check_vma=False,
    )
```

```python
import jax
import jax.numpy as jnp
from jax import lax
from jax.experimental import pallas as pl
from jax.experimental.pallas import tpu as pltpu
from jax.sharding import PartitionSpec as P


DT = 0.01
DENSITY = 240.0
SC = 20.0
NB = 8
NP = 26
NT = NB * NP
U = 8
LAG = 2

f32 = jnp.float32
bf16 = jnp.bfloat16
i32 = jnp.int32


def passed_along(x, axis, by):
    peers = lax.axis_size(axis)
    return lax.ppermute(x, axis, [(i, (i + by) % peers) for i in range(peers)])


def embed_kernel(home_ref, lent_ref, x_ref, out, slots):
    out[0:13] = x_ref[...]
    row = lax.broadcasted_iota(i32, (NB, 128), 0)
    home = jnp.zeros((NB, 128), i32)
    for b in range(NB):
        home = jnp.where(row == b, home_ref[0, b], home)
    out[13] = home.astype(f32)
    slots[...] = jnp.where(row == 0, lent_ref[0, 0], lent_ref[0, 1]).astype(f32)


def pick(x, slots, out, at):
    row = lax.broadcasted_iota(i32, (NB, 128), 0).astype(f32)
    for q in range(2):
        chosen = row == jnp.broadcast_to(slots[q : q + 1, :], (NB, 128))
        for c in range(13):
            out[at + 16 * q + c : at + 16 * q + c + 1, :] = jnp.sum(
                jnp.where(chosen, x[c], 0.0), 0, keepdims=True
            )
        out[at + 16 * q + 13 : at + 16 * q + 16, :] = jnp.zeros((3, 128), f32)


def sort_kernel(mine, past, slots, next_slots, keep, ship, lent, lent_next):
    me = lax.axis_index("gx").astype(i32)
    row = lax.broadcasted_iota(i32, (NB, 128), 0)
    here = (me * NB + row).astype(f32)
    there = (((me + 1) & 31) * NB + row).astype(f32)
    held = []
    for ref in (mine, past):
        for t in range(NB):
            home = ref[13] if t == 0 else pltpu.roll(ref[13], t, 0)
            held.append((ref, t, home == here, home == there))
    stays, goes = [], []
    for c in range(13):
        stay = jnp.zeros((NB, 128), f32)
        go = jnp.zeros((NB, 128), f32)
        for ref, t, is_here, is_there in held:
            x = ref[c] if t == 0 else pltpu.roll(ref[c], t, 0)
            stay = jnp.where(is_here, x, stay)
            go = jnp.where(is_there, x, go)
        stays.append(stay)
        goes.append(go)
    for x in (stays, goes):
        for c in range(3):
            x[c] = x[c] + DT * x[3 + c] + (0.5 * DT * DT) * x[9 + c]
    for c in range(13):
        keep[c] = stays[c]
        ship[8 * c : 8 * c + 8, :] = goes[c]
    pick(stays, slots, lent, 0)
    ship[104:136, :] = lent[...]
    pick(goes, next_slots, lent_next, 0)


def join_kernel(keep, came, far, fore, lent_next, slots, drifted, line):
    x = [keep[c] + came[8 * c : 8 * c + 8, :] for c in range(13)]
    for c in range(13):
        drifted[c] = x[c]
    line[0:32, :] = came[104:136, :] + far[...]
    pick(x, slots, line, 32)
    line[64:96, :] = fore[...] + lent_next[...]


def list_kernel(count_ref, pairs_ref, out_ref, out, sem):
    lane = lax.broadcasted_iota(i32, (1, 256), 1)
    code = jnp.where(lane < count_ref[0, 0], pairs_ref[1:2, :] * NB + pairs_ref[0:1, :], 255)
    rows = 224
    c = lax.broadcasted_iota(i32, (rows, 256), 0)
    hit = jnp.where(code == c, 1.0, 0.0).astype(bf16)
    often = jnp.dot(hit, jnp.ones((256, 128), bf16), preferred_element_type=f32)
    ci = lax.broadcasted_iota(i32, (rows, 128), 0)
    there = (often > 0.5) & (ci < NT)
    r = lax.broadcasted_iota(i32, (rows, rows), 0)
    q = lax.broadcasted_iota(i32, (rows, rows), 1)
    rank = jnp.dot(
        jnp.where(q < r, 1.0, 0.0).astype(bf16),
        jnp.where(there, 1.0, 0.0).astype(bf16),
        preferred_element_type=f32,
    )
    cf = ci.astype(f32)
    for half in range(2):
        e = lax.broadcasted_iota(i32, (rows, 128), 1).astype(f32) + 128.0 * half
        pick = there & (rank == e)
        sl = slice(128 * half, 128 * half + 128)
        out[0:1, sl] = jnp.sum(jnp.where(pick, cf, 0.0), 0, keepdims=True).astype(i32)
        out[1:2, sl] = jnp.sum(jnp.where(pick, often, 0.0), 0, keepdims=True).astype(i32)
        out[2:3, sl] = rank[64:65].astype(i32)
        out[3:4, sl] = rank[NT : NT + 1].astype(i32)
    copy = pltpu.make_async_copy(out, out_ref, sem)
    copy.start()
    copy.wait()


def split3(f):
    h = f.astype(bf16)
    r = f - h.astype(f32)
    m = r.astype(bf16)
    return h, m, (r - m.astype(f32)).astype(bf16)


def cross(a, b):
    return [
        a[1] * b[2] - a[2] * b[1],
        a[2] * b[0] - a[0] * b[2],
        a[0] * b[1] - a[1] * b[0],
    ]


def dot3(a, b):
    return a[0] * b[0] + a[1] * b[1] + a[2] * b[2]


def scaled(get):
    x = [get(c) * SC for c in range(3)]
    v = [get(3 + c) for c in range(3)]
    r = get(12)
    u = [r * get(6 + c) for c in range(3)]
    return x, v, u, r * SC


def left_prep(get, ab, la, feat):
    x, v, u, rp = scaled(get)
    zero = jnp.zeros_like(rp)
    rows = x + v + u + [dot3(x, v), dot3(x, u), jnp.ones_like(rp), rp, zero, zero, zero]
    for n, q in enumerate(rows):
        feat[pl.ds(n, NB, stride=16), :] = q
    a = lax.broadcasted_iota(i32, (128, 128), 0)
    b = lax.broadcasted_iota(i32, (128, 128), 1)
    for i in range(NB):
        f = feat[16 * i : 16 * i + 16, :]
        h, m, l = (p.astype(f32) for p in split3(f))
        t = jnp.concatenate([h, h, m, m, h, l, f, jnp.zeros((16, 128), f32)], 0).T
        la[i] = jnp.where(b < 96, t, 0.0).astype(bf16)
        for n, c in enumerate((96, 97, 98, 108)):
            ab[i, n] = jnp.broadcast_to(t[:, c : c + 1], (128, 128))
        ab[i, 4] = jnp.where(a == b, 1e15, jnp.broadcast_to(t[:, 96:97], (128, 128)))


def right_prep(get, nb, at, rb, kb, wb, feat):
    x, v, u, rp = scaled(get)
    one = jnp.ones_like(rp)
    zero = jnp.zeros_like(rp)
    neg = lambda a: [-q for q in a]
    sb = jnp.sqrt(rp)
    s = neg(v) + neg(x) + [zero] * 3 + [one, zero, dot3(x, v)]
    t = u + [zero] * 3 + neg(x) + [zero, one, -dot3(x, u)]
    w = [sb * q for q in [one] + x + v + u + cross(u, x) + cross(x, v)]
    for k, rows in enumerate((s, t, w, x + [rp])):
        for n in range(16 if k < 3 else 4):
            feat[pl.ds(128 * k + n, nb, stride=16), :] = rows[n] if n < len(rows) else zero
    for p in range(nb):
        j = at[p]
        fs, ft, fw = (feat[128 * k + 16 * p : 128 * k + 16 * p + 16, :] for k in range(3))
        rb[j] = feat[384 + 16 * p : 384 + 16 * p + 8, :]
        sh, sm, sl = split3(fs)
        th, tm, tl = split3(ft)
        for n, (p0, p1) in enumerate(
            ((sh, th), (sm, tm), (sh, th), (sm, tm), (sl, tl), (sh, th))
        ):
            kb[j, 16 * n : 16 * n + 16, 0:128] = p0
            kb[j, 16 * n : 16 * n + 16, 128:256] = p1
        kb[j, 96:128, :] = jnp.zeros((32, 256), bf16)
        for n, p0 in enumerate(split3(fw)):
            wb[j, 16 * n : 16 * n + 16, 0:128] = p0
            wb[j, 16 * n : 16 * n + 16, 128:256] = p0


def tile_dots(i, j, la, kb, st):
    st[...] = jnp.dot(la[i], kb[j], preferred_element_type=f32)


def tile_terms(i, j, same, ab, st, rb, cf):
    xi = jnp.where(same, 4, 0)
    rows = 16
    right = [jnp.broadcast_to(rb[j, q : q + 1, :], (rows, 128)) for q in range(4)]
    for c in range(128 // rows):
        sl = slice(rows * c, rows * c + rows)
        dx = ab[i, xi, sl, :] - right[0]
        dy = ab[i, 1, sl, :] - right[1]
        dz = ab[i, 2, sl, :] - right[2]
        rs = ab[i, 3, sl, :] + right[3]
        d2 = jnp.minimum(dx * dx + dy * dy + dz * dz, 1e37)
        inv = lax.rsqrt(d2)
        depth = jnp.maximum(rs - d2 * inv, 0.0)
        rc = depth * lax.rsqrt(jnp.maximum(depth * rs, 1e-35))
        ga = rc * inv
        gi = ga * inv
        al = ga * depth - gi * st[sl, 0:128]
        de = gi * st[sl, 128:256]
        for n, co in enumerate((al, rc, ga, de)):
            h = co.astype(bf16)
            at = 128 * n + rows * c
            cf[at : at + rows, :] = h
            cf[512 + at : 512 + at + rows, :] = (co - h.astype(f32)).astype(bf16)


def tile_sums(i, j, mult, wb, cf, acc):
    both = jnp.concatenate([cf[0:512, :], cf[512:1024, :]], 1)
    o = lax.dot_general(wb[j], both, (((1,), (1,)), ((), ())), preferred_element_type=f32)
    o = (o[0:16] + o[16:32] + o[32:48]) * mult
    for q in range(4):
        at = pl.ds(pl.multiple_of(i * 16, 16) + 128 * q, 16)
        acc[at, :] = acc[at, :] + o[:, 128 * q : 128 * q + 128]


def tile_loop(start, stop, list_ref, ab, la, rb, kb, wb, cfs, sts, acc, base_j=0):
    def get(e):
        live = e < stop
        code = jnp.where(live, list_ref[0, e], 8 * base_j)
        often = jnp.where(live, list_ref[1, e], 0)
        return code & 7, (code >> 3) - base_j, often.astype(f32)

    trips = (stop - start + U - 1) // U
    for n in range(U - LAG, U):
        cfs[n][...] = jnp.zeros_like(cfs[n])
    for n in range(U):
        i, j, _ = get(start + n)
        tile_dots(i, j, la, kb, sts[n])

    def body(t, late):
        base = start + U * t
        late = list(late)
        for n in range(U):
            i, j, mult = get(base + n)
            tile_terms(i, j, i == j + base_j, ab, sts[n], rb, cfs[n])
            late.append((i, j, mult))
            i, j, mult = late.pop(0)
            tile_sums(i, j, mult, wb, cfs[(n - LAG) % U], acc)
            i, j, _ = get(base + U + n)
            tile_dots(i, j, la, kb, sts[n])
        return tuple(late)

    none = (jnp.int32(0), jnp.int32(0), jnp.float32(0))
    late = lax.fori_loop(0, trips, body, (none,) * LAG)
    for n, (i, j, mult) in enumerate(late):
        tile_sums(i, j, mult, wb, cfs[U - LAG + n], acc)


def own_kernel(list_ref, d, ab, la, acc, rb, kb, wb, feat, *bufs):
    left_prep(lambda c: d[c], ab, la, feat)
    right_prep(lambda c: d[c], NB, range(NB), rb, kb, wb, feat)
    acc[...] = jnp.zeros_like(acc)
    tile_loop(jnp.int32(0), list_ref[2, 0], list_ref, ab, la, rb, kb, wb, bufs[:U], bufs[U:], acc)


def ghost_kernel(list_ref, d, ab, la, part, below, line, above, out, acc, rb, kb, wb, feat, *bufs):
    acc[...] = part[...]
    for ref, lo in ((below, 0), (line, 6), (above, 12)):
        right_prep(lambda c: ref[pl.ds(c, 6, stride=16), :], 6, range(lo, lo + 6), rb, kb, wb, feat)
    tile_loop(
        list_ref[2, 0], list_ref[3, 0], list_ref, ab, la, rb, kb, wb, bufs[:U], bufs[U:], acc, NB
    )
    finish(d, acc, out)


def finish(d, acc, out):
    need = (4, 10, 16, 4)
    a, b, g, e = (
        [acc[pl.ds(128 * q + r, NB, stride=16), :] for r in range(need[q])]
        for q in range(4)
    )
    x, v, u, rp = scaled(lambda c: d[c])
    uxg = cross(u, g[1:4])
    ux = cross(u, x)
    gux = cross(g[7:10], x)
    xv = cross(x, v)
    xgv = cross(x, g[4:7])
    gxv = cross(g[1:4], v)
    r = d[12]
    mass = (DENSITY * (4.0 / 3.0) * jnp.pi) * (r * r * r)
    inertia = 0.4 * mass * r * r
    half = 0.5 * jnp.sqrt(rp)
    to_acc = half / mass
    to_ang = half * r * DT / inertia
    for c in range(3):
        force = (
            x[c] * (a[0] - g[0])
            - (a[1 + c] - g[1 + c])
            - (v[c] * b[0] - b[4 + c])
            + (ux[c] * g[0] - uxg[c] + gux[c] - g[10 + c])
        )
        torque = (
            (xv[c] * g[0] - xgv[c] - gxv[c] + g[13 + c])
            - (u[c] * b[0] + b[7 + c])
            + (x[c] * e[0] - e[1 + c])
        )
        accel = force * to_acc
        if c == 2:
            accel = accel - 1.0
        out[c] = d[c]
        out[3 + c] = v[c] + (0.5 * DT) * (d[9 + c] + accel)
        out[6 + c] = d[6 + c] + torque * to_ang
        out[9 + c] = accel
    out[12] = r


VM = pl.BlockSpec(memory_space=pltpu.VMEM)
SM = pl.BlockSpec(memory_space=pltpu.SMEM)


def kernel_call(body, ins, outs, scratch=()):
    kinds = {"smem": pltpu.SMEM, "vmem": pltpu.VMEM, "sfar": pltpu.HBM, "hbm": pltpu.HBM}
    args = [
        pltpu.with_memory_space_constraint(x, kinds[space]) if space in kinds else x
        for x, space in ins
    ]
    return pl.pallas_call(
        body,
        out_shape=outs,
        in_specs=[SM if space in ("smem", "sfar", "scalar") else VM for _, space in ins],
        out_specs=tuple(
            SM if getattr(o, "memory_space", None) == pltpu.SMEM else VM for o in outs
        ),
        scratch_shapes=list(scratch),
        compiler_params=pltpu.CompilerParams(vmem_limit_bytes=16 << 20),
    )(*args)


WORK = [pltpu.VMEM((1024, 128), bf16)] * U + [pltpu.VMEM((128, 256), f32)] * U
FEAT = pltpu.VMEM((512, 128), f32)
SUMS = pltpu.VMEM((4 * NB * 16, 128), f32)


def right_refs(n):
    return [
        pltpu.VMEM((n, 8, 128), f32),
        pltpu.VMEM((n, 128, 256), bf16),
        pltpu.VMEM((n, 48, 256), bf16),
        FEAT,
    ]


def own_call(order, drifted):
    return kernel_call(
        own_kernel,
        [(order, "smem"), (drifted, "vmem")],
        (pltpu.VMEM((NB, 5, 128, 128), f32), pltpu.VMEM((NB, 128, 128), bf16), SUMS),
        right_refs(NB) + WORK,
    )


def ghost_call(order, drifted, made, below, line, above):
    ab, la, part = made
    (out,) = kernel_call(
        ghost_kernel,
        [(order, "smem")] + [(x, "vmem") for x in (drifted, ab, la, part, below, line, above)],
        (jax.ShapeDtypeStruct((13, NB, 128), f32),),
        [SUMS] + right_refs(18) + WORK,
    )
    return out


def one_step(spheres, new_home, ghost_list, tile_pairs, tile_count):
    block = pltpu.VMEM((13, NB, 128), f32)
    pair = pltpu.VMEM((32, 128), f32)
    mine, slots = kernel_call(
        embed_kernel,
        [(new_home, "sfar"), (ghost_list, "sfar"), (spheres.reshape(13, NB, 128), "hbm")],
        (pltpu.VMEM((14, NB, 128), f32), pltpu.VMEM((NB, 128), f32)),
    )
    past = passed_along(mine, "gx", 2)
    next_slots = passed_along(slots, "gx", -1)
    (order,) = kernel_call(
        list_kernel,
        [(tile_count, "scalar"), (tile_pairs[0].T, "hbm")],
        (pltpu.SMEM((8, 256), i32),),
        [pltpu.VMEM((8, 256), i32), pltpu.SemaphoreType.DMA(())],
    )
    order, past, next_slots = lax.optimization_barrier((order, past, next_slots))
    keep, ship, lent, lent_next = kernel_call(
        sort_kernel,
        [(x, "vmem") for x in (mine, past, slots, next_slots)],
        (block, pltpu.VMEM((136, 128), f32), pair, pair),
    )
    far = passed_along(lent_next, "gx", 2)
    came = passed_along(ship, "gx", 1)
    fore = passed_along(lent, "gx", -1)
    drifted, line = kernel_call(
        join_kernel,
        [(x, "vmem") for x in (keep, came, far, fore, lent_next, slots)],
        (block, pltpu.VMEM((96, 128), f32)),
    )
    below = passed_along(line, "gy", 1)
    above = passed_along(line, "gy", -1)
    made = own_call(order, drifted)
    return ghost_call(order, drifted, made, below, line, above)[:, None]


def solution(mesh):
    in_specs = (
        P(None, "gy", "gx", None),
        P("gy", "gx"),
        P("gy", "gx"),
        P("gy", "gx", None),
        P("gy", "gx"),
    )
    return jax.shard_map(
        one_step,
        mesh=mesh,
        in_specs=in_specs,
        out_specs=P(None, "gy", "gx", None),
        check_vma=False,
    )
```

```python
import jax
import jax.numpy as jnp
from jax import lax
from jax.experimental import pallas as pl
from jax.experimental.pallas import tpu as pltpu
from jax.sharding import PartitionSpec as P


DT = 0.01
DENSITY = 240.0
SC = 20.0
NB = 8
NP = 26
NT = NB * NP
U = 12
AHEAD = 2
LAG = 1

f32 = jnp.float32
bf16 = jnp.bfloat16
i32 = jnp.int32


def passed_along(x, axis, by):
    peers = lax.axis_size(axis)
    return lax.ppermute(x, axis, [(i, (i + by) % peers) for i in range(peers)])


def embed_kernel(home_ref, lent_ref, x_ref, out, slots):
    out[0:13] = x_ref[...]
    row = lax.broadcasted_iota(i32, (NB, 128), 0)
    home = jnp.zeros((NB, 128), i32)
    for b in range(NB):
        home = jnp.where(row == b, home_ref[0, b], home)
    out[13] = home.astype(f32)
    slots[...] = jnp.where(row == 0, lent_ref[0, 0], lent_ref[0, 1]).astype(f32)


def pick(x, slots, out, at):
    row = lax.broadcasted_iota(i32, (NB, 128), 0).astype(f32)
    for q in range(2):
        chosen = row == jnp.broadcast_to(slots[q : q + 1, :], (NB, 128))
        for c in range(13):
            out[at + 16 * q + c : at + 16 * q + c + 1, :] = jnp.sum(
                jnp.where(chosen, x[c], 0.0), 0, keepdims=True
            )
        out[at + 16 * q + 13 : at + 16 * q + 16, :] = jnp.zeros((3, 128), f32)


def sort_kernel(mine, past, slots, next_slots, keep, ship, lent, lent_next):
    me = lax.axis_index("gx").astype(i32)
    row = lax.broadcasted_iota(i32, (NB, 128), 0)
    here = (me * NB + row).astype(f32)
    there = (((me + 1) & 31) * NB + row).astype(f32)
    held = []
    for ref in (mine, past):
        for t in range(NB):
            home = ref[13] if t == 0 else pltpu.roll(ref[13], t, 0)
            held.append((ref, t, home == here, home == there))
    stays, goes = [], []
    for c in range(13):
        stay = jnp.zeros((NB, 128), f32)
        go = jnp.zeros((NB, 128), f32)
        for ref, t, is_here, is_there in held:
            x = ref[c] if t == 0 else pltpu.roll(ref[c], t, 0)
            stay = jnp.where(is_here, x, stay)
            go = jnp.where(is_there, x, go)
        stays.append(stay)
        goes.append(go)
    for x in (stays, goes):
        for c in range(3):
            x[c] = x[c] + DT * x[3 + c] + (0.5 * DT * DT) * x[9 + c]
    for c in range(13):
        keep[c] = stays[c]
        ship[8 * c : 8 * c + 8, :] = goes[c]
    pick(stays, slots, lent, 0)
    ship[104:136, :] = lent[...]
    pick(goes, next_slots, lent_next, 0)


def join_kernel(keep, came, far, fore, lent_next, slots, drifted, line):
    x = [keep[c] + came[8 * c : 8 * c + 8, :] for c in range(13)]
    for c in range(13):
        drifted[c] = x[c]
    line[0:32, :] = came[104:136, :] + far[...]
    pick(x, slots, line, 32)
    line[64:96, :] = fore[...] + lent_next[...]


def list_kernel(count_ref, pairs_ref, out_ref, out, sem):
    lane = lax.broadcasted_iota(i32, (1, 256), 1)
    code = jnp.where(lane < count_ref[0, 0], pairs_ref[1:2, :] * NB + pairs_ref[0:1, :], 255)
    rows = 224
    c = lax.broadcasted_iota(i32, (rows, 256), 0)
    hit = jnp.where(code == c, 1.0, 0.0).astype(bf16)
    often = jnp.dot(hit, jnp.ones((256, 128), bf16), preferred_element_type=f32)
    co = lax.broadcasted_iota(i32, (64, 256), 0)
    mirror = jnp.dot(
        jnp.where(code == ((co & 7) << 3) + (co >> 3), 1.0, 0.0).astype(bf16),
        jnp.ones((256, 128), bf16),
        preferred_element_type=f32,
    )
    mirror = jnp.concatenate([mirror, jnp.zeros((rows - 64, 128), f32)], 0)
    ci = lax.broadcasted_iota(i32, (rows, 128), 0)
    first, second = ci & 7, ci >> 3
    mirror = jnp.where(first < second, mirror, 0.0)
    there = (often + mirror > 0.5) & (ci < NT) & (first <= second)
    r = lax.broadcasted_iota(i32, (rows, rows), 0)
    q = lax.broadcasted_iota(i32, (rows, rows), 1)
    rank = jnp.dot(
        jnp.where(q < r, 1.0, 0.0).astype(bf16),
        jnp.where(there, 1.0, 0.0).astype(bf16),
        preferred_element_type=f32,
    )
    cf = ci.astype(f32)
    for half in range(2):
        e = lax.broadcasted_iota(i32, (rows, 128), 1).astype(f32) + 128.0 * half
        pick = there & (rank == e)
        sl = slice(128 * half, 128 * half + 128)
        out[0:1, sl] = jnp.sum(jnp.where(pick, cf, 0.0), 0, keepdims=True).astype(i32)
        out[1:2, sl] = jnp.sum(jnp.where(pick, often, 0.0), 0, keepdims=True).astype(i32)
        out[2:3, sl] = jnp.sum(jnp.where(pick, mirror, 0.0), 0, keepdims=True).astype(i32)
        out[3:4, sl] = rank[64:65].astype(i32)
        out[4:5, sl] = rank[NT : NT + 1].astype(i32)
    copy = pltpu.make_async_copy(out, out_ref, sem)
    copy.start()
    copy.wait()


def split3(f):
    h = f.astype(bf16)
    r = f - h.astype(f32)
    m = r.astype(bf16)
    return h, m, (r - m.astype(f32)).astype(bf16)


def cross(a, b):
    return [
        a[1] * b[2] - a[2] * b[1],
        a[2] * b[0] - a[0] * b[2],
        a[0] * b[1] - a[1] * b[0],
    ]


def dot3(a, b):
    return a[0] * b[0] + a[1] * b[1] + a[2] * b[2]


def scaled(get):
    x = [get(c) * SC for c in range(3)]
    v = [get(3 + c) for c in range(3)]
    r = get(12)
    u = [r * get(6 + c) for c in range(3)]
    return x, v, u, r * SC


def left_prep(get, ab, la, feat):
    x, v, u, rp = scaled(get)
    zero = jnp.zeros_like(rp)
    rows = x + v + u + [dot3(x, v), dot3(x, u), jnp.ones_like(rp), rp, zero, zero, zero]
    for n, q in enumerate(rows):
        feat[pl.ds(n, NB, stride=16), :] = q
    a = lax.broadcasted_iota(i32, (128, 128), 0)
    b = lax.broadcasted_iota(i32, (128, 128), 1)
    for i in range(NB):
        f = feat[16 * i : 16 * i + 16, :]
        h, m, l = (p.astype(f32) for p in split3(f))
        t = jnp.concatenate([h, h, m, m, h, l, f, jnp.zeros((16, 128), f32)], 0).T
        la[i] = jnp.where(b < 96, t, 0.0).astype(bf16)
        for n, c in enumerate((96, 97, 98, 108)):
            ab[i, n] = jnp.broadcast_to(t[:, c : c + 1], (128, 128))
        ab[i, 4] = jnp.where(a == b, 1e15, jnp.broadcast_to(t[:, 96:97], (128, 128)))


def right_prep(get, nb, at, rb, kb, wb, feat):
    x, v, u, rp = scaled(get)
    one = jnp.ones_like(rp)
    zero = jnp.zeros_like(rp)
    neg = lambda a: [-q for q in a]
    sb = jnp.sqrt(rp)
    s = neg(v) + neg(x) + [zero] * 3 + [one, zero, dot3(x, v)]
    t = u + [zero] * 3 + neg(x) + [zero, one, -dot3(x, u)]
    w = [sb * q for q in [one] + x + v + u + cross(u, x) + cross(x, v)]
    for k, rows in enumerate((s, t, w, x + [rp])):
        for n in range(16 if k < 3 else 4):
            feat[pl.ds(128 * k + n, nb, stride=16), :] = rows[n] if n < len(rows) else zero
    for p in range(nb):
        j = at[p]
        fs, ft, fw = (feat[128 * k + 16 * p : 128 * k + 16 * p + 16, :] for k in range(3))
        rb[j] = feat[384 + 16 * p : 384 + 16 * p + 8, :]
        sh, sm, sl = split3(fs)
        th, tm, tl = split3(ft)
        for n, (p0, p1) in enumerate(
            ((sh, th), (sm, tm), (sh, th), (sm, tm), (sl, tl), (sh, th))
        ):
            kb[j, 16 * n : 16 * n + 16, 0:128] = p0
            kb[j, 16 * n : 16 * n + 16, 128:256] = p1
        kb[j, 96:128, :] = jnp.zeros((32, 256), bf16)
        for n, p0 in enumerate(split3(fw)):
            wb[j, 16 * n : 16 * n + 16, 0:128] = p0
            wb[j, 16 * n : 16 * n + 16, 128:256] = p0


def tile_dots(i, j, la, kb, st):
    st[...] = jnp.dot(la[i], kb[j], preferred_element_type=f32)


def tile_terms(i, j, same, ab, st, rb, cf):
    xi = jnp.where(same, 4, 0)
    rows = 16
    right = [jnp.broadcast_to(rb[j, q : q + 1, :], (rows, 128)) for q in range(4)]
    for c in range(128 // rows):
        sl = slice(rows * c, rows * c + rows)
        dx = ab[i, xi, sl, :] - right[0]
        dy = ab[i, 1, sl, :] - right[1]
        dz = ab[i, 2, sl, :] - right[2]
        rs = ab[i, 3, sl, :] + right[3]
        d2 = jnp.minimum(dx * dx + dy * dy + dz * dz, 1e37)
        inv = lax.rsqrt(d2)
        depth = jnp.maximum(rs - d2 * inv, 0.0)
        rc = depth * lax.rsqrt(jnp.maximum(depth * rs, 1e-35))
        ga = rc * inv
        gi = ga * inv
        al = ga * depth - gi * st[sl, 0:128]
        de = gi * st[sl, 128:256]
        for n, co in enumerate((al, rc, ga, de)):
            h = co.astype(bf16)
            at = 128 * n + rows * c
            cf[at : at + rows, :] = h
            cf[512 + at : 512 + at + rows, :] = (co - h.astype(f32)).astype(bf16)


def add_sums(o, i, mult, acc, flip):
    o = o[0:16] + o[16:32] + o[32:48]
    for q in range(4):
        at = pl.ds(pl.multiple_of(i * 16, 16) + 128 * q, 16)
        part = o[:, 128 * q : 128 * q + 128] * mult
        acc[at, :] = acc[at, :] - part if flip and q == 3 else acc[at, :] + part


def tile_sums(i, j, mult, wb, cf, acc):
    both = jnp.concatenate([cf[0:512, :], cf[512:1024, :]], 1)
    o = lax.dot_general(wb[j], both, (((1,), (1,)), ((), ())), preferred_element_type=f32)
    add_sums(o, i, mult, acc, False)


def mirror_sums(i, j, mult, wb, cf, acc):
    cols = [
        jnp.concatenate([cf[128 * q : 128 * q + 128, :], cf[512 + 128 * q : 640 + 128 * q, :]], 0)
        for q in range(4)
    ]
    o = jnp.dot(wb[i], jnp.concatenate(cols, 1), preferred_element_type=f32)
    add_sums(o, j, mult, acc, True)


def tile_loop(start, stop, list_ref, ab, la, rb, kb, wb, cfs, sts, acc, base_j=0, both=False):
    def get(e):
        live = e < stop
        code = jnp.where(live, list_ref[0, e], 8 * base_j)
        often = jnp.where(live, list_ref[1, e], 0)
        mirror = jnp.where(live, list_ref[2, e], 0) if both else 0
        return code & 7, (code >> 3) - base_j, often.astype(f32), jnp.asarray(mirror, f32)

    def sums(tile, cf):
        i, j, mult, mirror = tile
        tile_sums(i, j, mult, wb, cf, acc)
        if both:
            mirror_sums(i, j, mirror, wb, cf, acc)

    trips = (stop - start + U - 1) // U
    for n in range(U - LAG, U):
        cfs[n][...] = jnp.zeros_like(cfs[n])
    for n in range(AHEAD):
        i, j, _, _ = get(start + n)
        tile_dots(i, j, la, kb, sts[n])

    def body(t, late):
        base = start + U * t
        late = list(late)
        for n in range(U):
            tile = get(base + n)
            i, j = tile[:2]
            tile_terms(i, j, i == j + base_j, ab, sts[n], rb, cfs[n])
            late.append(tile)
            sums(late.pop(0), cfs[(n - LAG) % U])
            i, j, _, _ = get(base + n + AHEAD)
            tile_dots(i, j, la, kb, sts[(n + AHEAD) % U])
        return tuple(late)

    none = (jnp.int32(0), jnp.int32(0), jnp.float32(0), jnp.float32(0))
    late = lax.fori_loop(0, trips, body, (none,) * LAG)
    for n, tile in enumerate(late):
        sums(tile, cfs[U - LAG + n])


def own_kernel(list_ref, d, ab, la, acc, rb, kb, wb, feat, *bufs):
    left_prep(lambda c: d[c], ab, la, feat)
    right_prep(lambda c: d[c], NB, range(NB), rb, kb, wb, feat)
    acc[...] = jnp.zeros_like(acc)
    tile_loop(
        jnp.int32(0), list_ref[3, 0], list_ref, ab, la, rb, kb, wb, bufs[:U], bufs[U:], acc, both=True
    )


def ghost_kernel(list_ref, d, ab, la, part, below, line, above, out, acc, rb, kb, wb, feat, *bufs):
    acc[...] = part[...]
    for ref, lo in ((below, 0), (line, 6), (above, 12)):
        right_prep(lambda c: ref[pl.ds(c, 6, stride=16), :], 6, range(lo, lo + 6), rb, kb, wb, feat)
    tile_loop(
        list_ref[3, 0], list_ref[4, 0], list_ref, ab, la, rb, kb, wb, bufs[:U], bufs[U:], acc, NB
    )
    finish(d, acc, out)


def finish(d, acc, out):
    need = (4, 10, 16, 4)
    a, b, g, e = (
        [acc[pl.ds(128 * q + r, NB, stride=16), :] for r in range(need[q])]
        for q in range(4)
    )
    x, v, u, rp = scaled(lambda c: d[c])
    uxg = cross(u, g[1:4])
    ux = cross(u, x)
    gux = cross(g[7:10], x)
    xv = cross(x, v)
    xgv = cross(x, g[4:7])
    gxv = cross(g[1:4], v)
    r = d[12]
    mass = (DENSITY * (4.0 / 3.0) * jnp.pi) * (r * r * r)
    inertia = 0.4 * mass * r * r
    half = 0.5 * jnp.sqrt(rp)
    to_acc = half / mass
    to_ang = half * r * DT / inertia
    for c in range(3):
        force = (
            x[c] * (a[0] - g[0])
            - (a[1 + c] - g[1 + c])
            - (v[c] * b[0] - b[4 + c])
            + (ux[c] * g[0] - uxg[c] + gux[c] - g[10 + c])
        )
        torque = (
            (xv[c] * g[0] - xgv[c] - gxv[c] + g[13 + c])
            - (u[c] * b[0] + b[7 + c])
            + (x[c] * e[0] - e[1 + c])
        )
        accel = force * to_acc
        if c == 2:
            accel = accel - 1.0
        out[c] = d[c]
        out[3 + c] = v[c] + (0.5 * DT) * (d[9 + c] + accel)
        out[6 + c] = d[6 + c] + torque * to_ang
        out[9 + c] = accel
    out[12] = r


VM = pl.BlockSpec(memory_space=pltpu.VMEM)
SM = pl.BlockSpec(memory_space=pltpu.SMEM)


def kernel_call(body, ins, outs, scratch=()):
    kinds = {"smem": pltpu.SMEM, "vmem": pltpu.VMEM, "sfar": pltpu.HBM, "hbm": pltpu.HBM}
    args = [
        pltpu.with_memory_space_constraint(x, kinds[space]) if space in kinds else x
        for x, space in ins
    ]
    return pl.pallas_call(
        body,
        out_shape=outs,
        in_specs=[SM if space in ("smem", "sfar", "scalar") else VM for _, space in ins],
        out_specs=tuple(
            SM if getattr(o, "memory_space", None) == pltpu.SMEM else VM for o in outs
        ),
        scratch_shapes=list(scratch),
        compiler_params=pltpu.CompilerParams(vmem_limit_bytes=16 << 20),
    )(*args)


WORK = [pltpu.VMEM((1024, 128), bf16)] * U + [pltpu.VMEM((128, 256), f32)] * U
FEAT = pltpu.VMEM((512, 128), f32)
SUMS = pltpu.VMEM((4 * NB * 16, 128), f32)


def right_refs(n):
    return [
        pltpu.VMEM((n, 8, 128), f32),
        pltpu.VMEM((n, 128, 256), bf16),
        pltpu.VMEM((n, 48, 256), bf16),
        FEAT,
    ]


def own_call(order, drifted):
    return kernel_call(
        own_kernel,
        [(order, "smem"), (drifted, "vmem")],
        (pltpu.VMEM((NB, 5, 128, 128), f32), pltpu.VMEM((NB, 128, 128), bf16), SUMS),
        right_refs(NB) + WORK,
    )


def ghost_call(order, drifted, made, below, line, above):
    ab, la, part = made
    (out,) = kernel_call(
        ghost_kernel,
        [(order, "smem")] + [(x, "vmem") for x in (drifted, ab, la, part, below, line, above)],
        (jax.ShapeDtypeStruct((13, NB, 128), f32),),
        [SUMS] + right_refs(18) + WORK,
    )
    return out


def one_step(spheres, new_home, ghost_list, tile_pairs, tile_count):
    block = pltpu.VMEM((13, NB, 128), f32)
    pair = pltpu.VMEM((32, 128), f32)
    mine, slots = kernel_call(
        embed_kernel,
        [(new_home, "sfar"), (ghost_list, "sfar"), (spheres.reshape(13, NB, 128), "hbm")],
        (pltpu.VMEM((14, NB, 128), f32), pltpu.VMEM((NB, 128), f32)),
    )
    past = passed_along(mine, "gx", 2)
    next_slots = passed_along(slots, "gx", -1)
    (order,) = kernel_call(
        list_kernel,
        [(tile_count, "scalar"), (tile_pairs[0].T, "hbm")],
        (pltpu.SMEM((8, 256), i32),),
        [pltpu.VMEM((8, 256), i32), pltpu.SemaphoreType.DMA(())],
    )
    order, past, next_slots = lax.optimization_barrier((order, past, next_slots))
    keep, ship, lent, lent_next = kernel_call(
        sort_kernel,
        [(x, "vmem") for x in (mine, past, slots, next_slots)],
        (block, pltpu.VMEM((136, 128), f32), pair, pair),
    )
    far = passed_along(lent_next, "gx", 2)
    came = passed_along(ship, "gx", 1)
    fore = passed_along(lent, "gx", -1)
    drifted, line = kernel_call(
        join_kernel,
        [(x, "vmem") for x in (keep, came, far, fore, lent_next, slots)],
        (block, pltpu.VMEM((96, 128), f32)),
    )
    below = passed_along(line, "gy", 1)
    above = passed_along(line, "gy", -1)
    made = own_call(order, drifted)
    return ghost_call(order, drifted, made, below, line, above)[:, None]


def solution(mesh):
    in_specs = (
        P(None, "gy", "gx", None),
        P("gy", "gx"),
        P("gy", "gx"),
        P("gy", "gx", None),
        P("gy", "gx"),
    )
    return jax.shard_map(
        one_step,
        mesh=mesh,
        in_specs=in_specs,
        out_specs=P(None, "gy", "gx", None),
        check_vma=False,
    )
```

```python
import jax
import jax.numpy as jnp
from jax import lax
from jax.experimental import pallas as pl
from jax.experimental.pallas import tpu as pltpu
from jax.sharding import PartitionSpec as P


DT = 0.01
DENSITY = 240.0
SC = 20.0
NB = 8
NP = 26
NT = NB * NP
OWN_U = 12
GHOST_U = 16
AHEAD = 2
LAG = 1

f32 = jnp.float32
bf16 = jnp.bfloat16
i32 = jnp.int32


def passed_along(x, axis, by):
    peers = lax.axis_size(axis)
    return lax.ppermute(x, axis, [(i, (i + by) % peers) for i in range(peers)])


def embed_kernel(home_ref, lent_ref, x_ref, out, slots):
    out[0:13] = x_ref[...]
    row = lax.broadcasted_iota(i32, (NB, 128), 0)
    home = jnp.zeros((NB, 128), i32)
    for b in range(NB):
        home = jnp.where(row == b, home_ref[0, b], home)
    out[13] = home.astype(f32)
    slots[...] = jnp.where(row == 0, lent_ref[0, 0], lent_ref[0, 1]).astype(f32)


def pick(x, slots, out, at):
    row = lax.broadcasted_iota(i32, (NB, 128), 0).astype(f32)
    for q in range(2):
        chosen = row == jnp.broadcast_to(slots[q : q + 1, :], (NB, 128))
        for c in range(13):
            out[at + 16 * q + c : at + 16 * q + c + 1, :] = jnp.sum(
                jnp.where(chosen, x[c], 0.0), 0, keepdims=True
            )
        out[at + 16 * q + 13 : at + 16 * q + 16, :] = jnp.zeros((3, 128), f32)


def sort_kernel(mine, past, slots, next_slots, keep, ship, lent, lent_next):
    me = lax.axis_index("gx").astype(i32)
    row = lax.broadcasted_iota(i32, (NB, 128), 0)
    here = (me * NB + row).astype(f32)
    there = (((me + 1) & 31) * NB + row).astype(f32)
    held = []
    for ref in (mine, past):
        for t in range(NB):
            home = ref[13] if t == 0 else pltpu.roll(ref[13], t, 0)
            held.append((ref, t, home == here, home == there))
    stays, goes = [], []
    for c in range(13):
        stay = jnp.zeros((NB, 128), f32)
        go = jnp.zeros((NB, 128), f32)
        for ref, t, is_here, is_there in held:
            x = ref[c] if t == 0 else pltpu.roll(ref[c], t, 0)
            stay = jnp.where(is_here, x, stay)
            go = jnp.where(is_there, x, go)
        stays.append(stay)
        goes.append(go)
    for x in (stays, goes):
        for c in range(3):
            x[c] = x[c] + DT * x[3 + c] + (0.5 * DT * DT) * x[9 + c]
    for c in range(13):
        keep[c] = stays[c]
        ship[8 * c : 8 * c + 8, :] = goes[c]
    pick(stays, slots, lent, 0)
    ship[104:136, :] = lent[...]
    pick(goes, next_slots, lent_next, 0)


def join_kernel(keep, came, far, fore, lent_next, slots, drifted, line):
    x = [keep[c] + came[8 * c : 8 * c + 8, :] for c in range(13)]
    for c in range(13):
        drifted[c] = x[c]
    line[0:32, :] = came[104:136, :] + far[...]
    pick(x, slots, line, 32)
    line[64:96, :] = fore[...] + lent_next[...]


def list_kernel(count_ref, pairs_ref, out_ref, out, sem):
    lane = lax.broadcasted_iota(i32, (1, 256), 1)
    code = jnp.where(lane < count_ref[0, 0], pairs_ref[1:2, :] * NB + pairs_ref[0:1, :], 255)
    rows = 224
    c = lax.broadcasted_iota(i32, (rows, 256), 0)
    hit = jnp.where(code == c, 1.0, 0.0).astype(bf16)
    often = jnp.dot(hit, jnp.ones((256, 128), bf16), preferred_element_type=f32)
    co = lax.broadcasted_iota(i32, (64, 256), 0)
    mirror = jnp.dot(
        jnp.where(code == ((co & 7) << 3) + (co >> 3), 1.0, 0.0).astype(bf16),
        jnp.ones((256, 128), bf16),
        preferred_element_type=f32,
    )
    mirror = jnp.concatenate([mirror, jnp.zeros((rows - 64, 128), f32)], 0)
    ci = lax.broadcasted_iota(i32, (rows, 128), 0)
    first, second = ci & 7, ci >> 3
    mirror = jnp.where(first < second, mirror, 0.0)
    there = (often + mirror > 0.5) & (ci < NT) & (first <= second)
    r = lax.broadcasted_iota(i32, (rows, rows), 0)
    q = lax.broadcasted_iota(i32, (rows, rows), 1)
    rank = jnp.dot(
        jnp.where(q < r, 1.0, 0.0).astype(bf16),
        jnp.where(there, 1.0, 0.0).astype(bf16),
        preferred_element_type=f32,
    )
    cf = ci.astype(f32)
    for half in range(2):
        e = lax.broadcasted_iota(i32, (rows, 128), 1).astype(f32) + 128.0 * half
        pick = there & (rank == e)
        sl = slice(128 * half, 128 * half + 128)
        out[0:1, sl] = jnp.sum(jnp.where(pick, cf, 0.0), 0, keepdims=True).astype(i32)
        out[1:2, sl] = jnp.sum(jnp.where(pick, often, 0.0), 0, keepdims=True).astype(i32)
        out[2:3, sl] = jnp.sum(jnp.where(pick, mirror, 0.0), 0, keepdims=True).astype(i32)
        out[3:4, sl] = rank[64:65].astype(i32)
        out[4:5, sl] = rank[NT : NT + 1].astype(i32)
    copy = pltpu.make_async_copy(out, out_ref, sem)
    copy.start()
    copy.wait()


def split3(f):
    h = f.astype(bf16)
    r = f - h.astype(f32)
    m = r.astype(bf16)
    return h, m, (r - m.astype(f32)).astype(bf16)


def cross(a, b):
    return [
        a[1] * b[2] - a[2] * b[1],
        a[2] * b[0] - a[0] * b[2],
        a[0] * b[1] - a[1] * b[0],
    ]


def dot3(a, b):
    return a[0] * b[0] + a[1] * b[1] + a[2] * b[2]


def scaled(get):
    x = [get(c) * SC for c in range(3)]
    v = [get(3 + c) for c in range(3)]
    r = get(12)
    u = [r * get(6 + c) for c in range(3)]
    return x, v, u, r * SC


def left_prep(get, ab, la, feat):
    x, v, u, rp = scaled(get)
    zero = jnp.zeros_like(rp)
    rows = x + v + u + [dot3(x, v), dot3(x, u), jnp.ones_like(rp), rp, zero, zero, zero]
    for n, q in enumerate(rows):
        feat[pl.ds(n, NB, stride=16), :] = q
    a = lax.broadcasted_iota(i32, (128, 128), 0)
    b = lax.broadcasted_iota(i32, (128, 128), 1)
    for i in range(NB):
        f = feat[16 * i : 16 * i + 16, :]
        h, m, l = (p.astype(f32) for p in split3(f))
        t = jnp.concatenate([h, h, m, m, h, l, f, jnp.zeros((16, 128), f32)], 0).T
        la[i] = jnp.where(b < 96, t, 0.0).astype(bf16)
        for n, c in enumerate((96, 97, 98, 108)):
            ab[i, n] = jnp.broadcast_to(t[:, c : c + 1], (128, 128))
        ab[i, 4] = jnp.where(a == b, 1e15, jnp.broadcast_to(t[:, 96:97], (128, 128)))


def right_prep(get, nb, at, rb, kb, wb, feat):
    x, v, u, rp = scaled(get)
    one = jnp.ones_like(rp)
    zero = jnp.zeros_like(rp)
    neg = lambda a: [-q for q in a]
    sb = jnp.sqrt(rp)
    s = neg(v) + neg(x) + [zero] * 3 + [one, zero, dot3(x, v)]
    t = u + [zero] * 3 + neg(x) + [zero, one, -dot3(x, u)]
    w = [sb * q for q in [one] + x + v + u + cross(u, x) + cross(x, v)]
    for k, rows in enumerate((s, t, w, x + [rp])):
        for n in range(16 if k < 3 else 4):
            feat[pl.ds(128 * k + n, nb, stride=16), :] = rows[n] if n < len(rows) else zero
    for p in range(nb):
        j = at[p]
        if j is None:
            continue
        fs, ft, fw = (feat[128 * k + 16 * p : 128 * k + 16 * p + 16, :] for k in range(3))
        rb[j] = feat[384 + 16 * p : 384 + 16 * p + 8, :]
        sh, sm, sl = split3(fs)
        th, tm, tl = split3(ft)
        for n, (p0, p1) in enumerate(
            ((sh, th), (sm, tm), (sh, th), (sm, tm), (sl, tl), (sh, th))
        ):
            kb[j, 16 * n : 16 * n + 16, 0:128] = p0
            kb[j, 16 * n : 16 * n + 16, 128:256] = p1
        kb[j, 96:128, :] = jnp.zeros((32, 256), bf16)
        for n, p0 in enumerate(split3(fw)):
            wb[j, 16 * n : 16 * n + 16, 0:128] = p0
            wb[j, 16 * n : 16 * n + 16, 128:256] = p0


def tile_dots(i, j, la, kb, st):
    st[...] = jnp.dot(la[i], kb[j], preferred_element_type=f32)


def tile_terms(i, j, same, ab, st, rb, cf):
    xi = jnp.where(same, 4, 0)
    rows = 16
    right = [jnp.broadcast_to(rb[j, q : q + 1, :], (rows, 128)) for q in range(4)]
    for c in range(128 // rows):
        sl = slice(rows * c, rows * c + rows)
        dx = ab[i, xi, sl, :] - right[0]
        dy = ab[i, 1, sl, :] - right[1]
        dz = ab[i, 2, sl, :] - right[2]
        rs = ab[i, 3, sl, :] + right[3]
        d2 = jnp.minimum(dx * dx + dy * dy + dz * dz, 1e37)
        inv = lax.rsqrt(d2)
        depth = jnp.maximum(rs - d2 * inv, 0.0)
        rc = depth * lax.rsqrt(jnp.maximum(depth * rs, 1e-35))
        ga = rc * inv
        gi = ga * inv
        al = ga * depth - gi * st[sl, 0:128]
        de = gi * st[sl, 128:256]
        for n, co in enumerate((al, rc, ga, de)):
            h = co.astype(bf16)
            at = 128 * n + rows * c
            cf[at : at + rows, :] = h
            cf[512 + at : 512 + at + rows, :] = (co - h.astype(f32)).astype(bf16)


def add_sums(o, i, mult, acc, flip):
    o = o[0:16] + o[16:32] + o[32:48]
    for q in range(4):
        at = pl.ds(pl.multiple_of(i * 16, 16) + 128 * q, 16)
        part = o[:, 128 * q : 128 * q + 128] * mult
        acc[at, :] = acc[at, :] - part if flip and q == 3 else acc[at, :] + part


def tile_sums(i, j, mult, wb, cf, acc):
    both = jnp.concatenate([cf[0:512, :], cf[512:1024, :]], 1)
    o = lax.dot_general(wb[j], both, (((1,), (1,)), ((), ())), preferred_element_type=f32)
    add_sums(o, i, mult, acc, False)


def mirror_sums(i, j, mult, wb, cf, acc):
    cols = [
        jnp.concatenate([cf[128 * q : 128 * q + 128, :], cf[512 + 128 * q : 640 + 128 * q, :]], 0)
        for q in range(4)
    ]
    o = jnp.dot(wb[i], jnp.concatenate(cols, 1), preferred_element_type=f32)
    add_sums(o, j, mult, acc, True)


def tile_loop(start, stop, list_ref, ab, la, rb, kb, wb, cfs, sts, acc, base_j=0, both=False):
    def get(e):
        live = e < stop
        code = jnp.where(live, list_ref[0, e], 8 * base_j)
        often = jnp.where(live, list_ref[1, e], 0)
        mirror = jnp.where(live, list_ref[2, e], 0) if both else 0
        return code & 7, (code >> 3) - base_j, often.astype(f32), jnp.asarray(mirror, f32)

    def sums(tile, cf):
        i, j, mult, mirror = tile
        tile_sums(i, j, mult, wb, cf, acc)
        if both:
            mirror_sums(i, j, mirror, wb, cf, acc)

    U = len(cfs)
    trips = (stop - start + U - 1) // U
    for n in range(U - LAG, U):
        cfs[n][...] = jnp.zeros_like(cfs[n])
    for n in range(AHEAD):
        i, j, _, _ = get(start + n)
        tile_dots(i, j, la, kb, sts[n])

    def body(t, late):
        base = start + U * t
        late = list(late)
        for n in range(U):
            tile = get(base + n)
            i, j = tile[:2]
            tile_terms(i, j, i == j + base_j, ab, sts[n], rb, cfs[n])
            late.append(tile)
            sums(late.pop(0), cfs[(n - LAG) % U])
            i, j, _, _ = get(base + n + AHEAD)
            tile_dots(i, j, la, kb, sts[(n + AHEAD) % U])
        return tuple(late)

    none = (jnp.int32(0), jnp.int32(0), jnp.float32(0), jnp.float32(0))
    late = lax.fori_loop(0, trips, body, (none,) * LAG)
    for n, tile in enumerate(late):
        sums(tile, cfs[U - LAG + n])


def own_kernel(list_ref, d, ab, la, acc, rb, kb, wb, feat, *bufs):
    left_prep(lambda c: d[c], ab, la, feat)
    right_prep(lambda c: d[c], NB, range(NB), rb, kb, wb, feat)
    acc[...] = jnp.zeros_like(acc)
    tile_loop(
        jnp.int32(0), list_ref[3, 0], list_ref, ab, la, rb, kb, wb, bufs[:OWN_U], bufs[OWN_U:], acc, both=True
    )


def ghost_kernel(list_ref, d, ab, la, part, below, line, above, out, acc, rb, kb, wb, feat, *bufs):
    acc[...] = part[...]
    for ref, at in (
        (below, (0, 1, 2, 3, 4, 5)),
        (line, (6, 7, None, None, 10, 11)),
        (above, (12, 13, 14, 15, 16, 17)),
    ):
        right_prep(lambda c: ref[pl.ds(c, 6, stride=16), :], 6, at, rb, kb, wb, feat)
    tile_loop(
        list_ref[3, 0], list_ref[4, 0], list_ref, ab, la, rb, kb, wb, bufs[:GHOST_U], bufs[GHOST_U:], acc, NB
    )
    finish(d, acc, out)


def finish(d, acc, out):
    need = (4, 10, 16, 4)
    a, b, g, e = (
        [acc[pl.ds(128 * q + r, NB, stride=16), :] for r in range(need[q])]
        for q in range(4)
    )
    x, v, u, rp = scaled(lambda c: d[c])
    uxg = cross(u, g[1:4])
    ux = cross(u, x)
    gux = cross(g[7:10], x)
    xv = cross(x, v)
    xgv = cross(x, g[4:7])
    gxv = cross(g[1:4], v)
    r = d[12]
    mass = (DENSITY * (4.0 / 3.0) * jnp.pi) * (r * r * r)
    inertia = 0.4 * mass * r * r
    half = 0.5 * jnp.sqrt(rp)
    to_acc = half / mass
    to_ang = half * r * DT / inertia
    for c in range(3):
        force = (
            x[c] * (a[0] - g[0])
            - (a[1 + c] - g[1 + c])
            - (v[c] * b[0] - b[4 + c])
            + (ux[c] * g[0] - uxg[c] + gux[c] - g[10 + c])
        )
        torque = (
            (xv[c] * g[0] - xgv[c] - gxv[c] + g[13 + c])
            - (u[c] * b[0] + b[7 + c])
            + (x[c] * e[0] - e[1 + c])
        )
        accel = force * to_acc
        if c == 2:
            accel = accel - 1.0
        out[c] = d[c]
        out[3 + c] = v[c] + (0.5 * DT) * (d[9 + c] + accel)
        out[6 + c] = d[6 + c] + torque * to_ang
        out[9 + c] = accel
    out[12] = r


VM = pl.BlockSpec(memory_space=pltpu.VMEM)
SM = pl.BlockSpec(memory_space=pltpu.SMEM)


def kernel_call(body, ins, outs, scratch=()):
    kinds = {"smem": pltpu.SMEM, "vmem": pltpu.VMEM, "sfar": pltpu.HBM, "hbm": pltpu.HBM}
    args = [
        pltpu.with_memory_space_constraint(x, kinds[space]) if space in kinds else x
        for x, space in ins
    ]
    return pl.pallas_call(
        body,
        out_shape=outs,
        in_specs=[SM if space in ("smem", "sfar", "scalar") else VM for _, space in ins],
        out_specs=tuple(
            SM if getattr(o, "memory_space", None) == pltpu.SMEM else VM for o in outs
        ),
        scratch_shapes=list(scratch),
        compiler_params=pltpu.CompilerParams(vmem_limit_bytes=16 << 20),
    )(*args)


def work(n):
    return [pltpu.VMEM((1024, 128), bf16)] * n + [pltpu.VMEM((128, 256), f32)] * n


FEAT = pltpu.VMEM((512, 128), f32)
SUMS = pltpu.VMEM((4 * NB * 16, 128), f32)


def right_refs(n):
    return [
        pltpu.VMEM((n, 8, 128), f32),
        pltpu.VMEM((n, 128, 256), bf16),
        pltpu.VMEM((n, 48, 256), bf16),
        FEAT,
    ]


def own_call(order, drifted):
    return kernel_call(
        own_kernel,
        [(order, "smem"), (drifted, "vmem")],
        (pltpu.VMEM((NB, 5, 128, 128), f32), pltpu.VMEM((NB, 128, 128), bf16), SUMS),
        right_refs(NB) + work(OWN_U),
    )


def ghost_call(order, drifted, made, below, line, above):
    ab, la, part = made
    (out,) = kernel_call(
        ghost_kernel,
        [(order, "smem")] + [(x, "vmem") for x in (drifted, ab, la, part, below, line, above)],
        (jax.ShapeDtypeStruct((13, NB, 128), f32),),
        [SUMS] + right_refs(18) + work(GHOST_U),
    )
    return out


def one_step(spheres, new_home, ghost_list, tile_pairs, tile_count):
    block = pltpu.VMEM((13, NB, 128), f32)
    pair = pltpu.VMEM((32, 128), f32)
    mine, slots = kernel_call(
        embed_kernel,
        [(new_home, "sfar"), (ghost_list, "sfar"), (spheres.reshape(13, NB, 128), "hbm")],
        (pltpu.VMEM((14, NB, 128), f32), pltpu.VMEM((NB, 128), f32)),
    )
    past = passed_along(mine, "gx", 2)
    next_slots = passed_along(slots, "gx", -1)
    (order,) = kernel_call(
        list_kernel,
        [(tile_count, "scalar"), (tile_pairs[0].T, "hbm")],
        (pltpu.SMEM((8, 256), i32),),
        [pltpu.VMEM((8, 256), i32), pltpu.SemaphoreType.DMA(())],
    )
    keep, ship, lent, lent_next = kernel_call(
        sort_kernel,
        [(x, "vmem") for x in (mine, past, slots, next_slots)],
        (block, pltpu.VMEM((136, 128), f32), pair, pair),
    )
    far = passed_along(lent_next, "gx", 2)
    came = passed_along(ship, "gx", 1)
    fore = passed_along(lent, "gx", -1)
    order, far, came, fore = lax.optimization_barrier((order, far, came, fore))
    drifted, line = kernel_call(
        join_kernel,
        [(x, "vmem") for x in (keep, came, far, fore, lent_next, slots)],
        (block, pltpu.VMEM((96, 128), f32)),
    )
    below = passed_along(line, "gy", 1)
    above = passed_along(line, "gy", -1)
    made = own_call(order, drifted)
    return ghost_call(order, drifted, made, below, line, above)[:, None]


def solution(mesh):
    in_specs = (
        P(None, "gy", "gx", None),
        P("gy", "gx"),
        P("gy", "gx"),
        P("gy", "gx", None),
        P("gy", "gx"),
    )
    return jax.shard_map(
        one_step,
        mesh=mesh,
        in_specs=in_specs,
        out_specs=P(None, "gy", "gx", None),
        check_vma=False,
    )
```
